32 devices in a mesh: dp: 8 (over y, x, core), fsdp: 4 (over z).
Axes of the slice: x: 2, y: 2, z: 4, core: 2. Of those that a mesh axis runs over, the one named last changes fastest.
Arguments:
- tokens: bfloat16 [16384, 1024], P(('dp', 'fsdp')), may hold values from -20 to 20
- w_qkv: bfloat16 [1024, 3072], P('fsdp'), may hold values from -0.1875 to 0.1875
- w_out: bfloat16 [1024, 1024], P('fsdp'), may hold values from -0.1875 to 0.1875
- doc_blocks: int32 [32, 4], P(('dp', 'fsdp')), may hold values from 0 to 1, never falling along the last dimension, each value on 1 to 3 neighbouring positions
- cotangent: bfloat16 [16384, 1024], P(('dp', 'fsdp')), may hold values from -6 to 6
Outputs:
- output: bfloat16 [16384, 1024], P(('dp', 'fsdp'))
- grad_tokens: bfloat16 [16384, 1024], P(('dp', 'fsdp'))
- grad_w_qkv: float32 [1024, 3072], P('fsdp')
- grad_w_out: float32 [1024, 1024], P('fsdp')
The draws below stay inside these ranges and needn't reach their ends.
Inputs may be any that keep to these rules, and one draw needn't show every extreme that they name: `doc_blocks`: ids never fall along a sequence; each of the 2 documents of a sequence covers 1 to 3 blocks.
All inputs are finite; a program needn't handle non-finite values.
Results may differ from the reference program's by a relative error of at most 0.012.
Values may be sent and summed in bfloat16 or wider, within the bound.
A program may use at most 128 MiB of HBM per device.

```python
import math
import jax
import jax.numpy as jnp
import numpy as np
from jax import lax

D = 1024
H = 8
HD = 128
TOK_DEV = 512
HW = 1024
NB = 4
DOCS = 2
MOST = 3
SEQS = 32
TOKENS = 16384


def draw_tokens(key, part):
    first = jax.random.fold_in(key, 0)
    values = jnp.clip(jax.random.normal(first, (TOKENS, D), jnp.float32), -6.0, 6.0)
    return values.astype(jnp.bfloat16)


def with_spikes(drawn, stream_key, source, target, shards_of, factor):
    owner, partner = [(jnp.arange(drawn.shape[dim]) // (drawn.shape[dim] // shards_of)).reshape([-1 if axis == dim else 1 for axis in range(drawn.ndim)]) for dim in (source, target)]
    chosen = jax.random.permutation(stream_key, shards_of)[partner]
    strong = (owner == chosen) | (owner == (partner + shards_of // 2) % shards_of)
    return jnp.where(strong, factor * drawn, drawn)


def steps_of(rng, dims, shards, least, top_value):
    level, own = 1.0, jax.random.fold_in(rng, 6)
    for dim, parts in shards:
        draws = jnp.exp(jax.random.uniform(jax.random.fold_in(own, dim), (parts,), jnp.float32, least / len(shards), top_value / len(shards)))
        level = level * jnp.repeat(draws, dims[dim] // parts).reshape([-1 if axis == dim else 1 for axis in range(len(dims))])
    return level


def length_profile(amount, total, reach, slope):
    portions = [(1 << 20) // math.isqrt(rank ** slope) + 1 for rank in range(2, amount + 1)]
    rest, given = total - reach - (amount - 1), [1] * (amount - 1)
    while rest > 0:
        candidates = [i for i in range(amount - 1) if given[i] < reach]
        pool, left = sum([portions[i] for i in candidates]), rest
        for i in candidates:
            extra = min(reach - given[i], max(1, left * portions[i] // pool), rest)
            given[i] = given[i] + extra
            rest = rest - extra
    return np.array([reach] + given)


def uneven_parts(key, number_of, total, reach, skew):
    if number_of == 2:
        one = jax.random.randint(key, (), max(1, total - reach), min(reach, total - 1) + 1)
        return jnp.stack([one, total - one])
    lengths = jnp.asarray(length_profile(number_of, total, reach, skew), jnp.int32)
    pairs = (number_of - 1) // 2
    giver, receiver = lengths[1:1 + 2 * pairs:2], lengths[2:2 + 2 * pairs:2]
    slack = jnp.minimum(giver - 1, reach - receiver)
    passed = jax.random.randint(jax.random.fold_in(key, 1), (pairs,), 0, 1 << 20) % (slack + 1)
    lengths = lengths.at[1:1 + 2 * pairs:2].set(giver - passed).at[2:2 + 2 * pairs:2].set(receiver + passed)
    return lengths[jax.random.permutation(jax.random.fold_in(key, 2), number_of)]


def centred(stream_key, shape, scale, reach, cuts=(), held_as=jnp.bfloat16):
    loudness = steps_of(stream_key, shape, cuts, -0.22, 0.18) if cuts else 1.0
    drawn = jax.random.normal(stream_key, shape, jnp.float32) * scale * loudness
    return jnp.minimum(jnp.maximum(drawn, -reach), reach).astype(held_as)


def noise_with(key, extent, spread, most, cuts, heavy, kind=jnp.bfloat16):
    entries = spread * jax.random.normal(key, extent, jnp.float32)
    if cuts:
        entries = entries * steps_of(key, extent, cuts, -0.22, 0.18)
    return jnp.clip(with_spikes(entries, jax.random.fold_in(key, 3), *heavy), -most, most).astype(kind)


def setup_inputs(seed: int = 0) -> dict:
    keys = jax.random.split(jax.random.key(seed), 6)
    tokens = draw_tokens(jax.random.fold_in(keys[5], 71), 0)
    w_qkv = centred(keys[1], (D, 3 * HW), D ** -0.5, 0.1875, ((0, 4),))
    w_out = centred(keys[2], (D, HW), HW ** -0.5, 0.1875, ((0, 4),))
    doc_blocks = jax.vmap(lambda own: jnp.searchsorted(jnp.cumsum(uneven_parts(own, DOCS, NB, MOST, 0)), jnp.arange(NB), side="right"))(jax.random.split(keys[3], SEQS)).reshape((SEQS, NB)).astype(jnp.int32)
    cotangent = noise_with(keys[4], (TOKENS, D), 1.0, 6.0, ((0, 32),), (0, 1, 32, 2.75))
    return {"tokens": tokens, "w_qkv": w_qkv, "w_out": w_out, "doc_blocks": doc_blocks, "cotangent": cotangent}


NEG_FILL = -1e+30

def row_mask(doc_ids, row_count):
    block_len = row_count // doc_ids.shape[0]
    doc_rows = jnp.repeat(doc_ids, block_len, total_repeat_length=row_count)
    position = jnp.arange(row_count, dtype=jnp.int32)
    causal = position[None, :] <= position[:, None]
    return causal & (doc_rows[None, :] == doc_rows[:, None])

def split_heads(matrix, head_count):
    return matrix.reshape(matrix.shape[0], head_count, matrix.shape[1] // head_count).astype(jnp.float32)

def attend_forward(query_rows, key_rows, value_rows, allowed, head_count):
    row_count = query_rows.shape[0]
    query_heads = split_heads(query_rows, head_count)
    key_heads = split_heads(key_rows, head_count)
    value_heads = split_heads(value_rows, head_count)
    score_scale = query_heads.shape[2] ** (-0.5)
    scores = jnp.einsum('qhd,khd->hqk', query_heads, key_heads, precision=lax.Precision.HIGHEST) * score_scale
    scores = jnp.where(allowed[None], scores, NEG_FILL)
    highest = lax.optimization_barrier(jnp.max(scores, axis=-1, keepdims=True))
    expvals = jnp.exp(scores - highest)
    attn_probs = expvals / lax.optimization_barrier(jnp.sum(expvals, axis=-1, keepdims=True))
    probs_half = attn_probs.astype(jnp.bfloat16)
    mixed = jnp.einsum('hqk,khd->qhd', probs_half.astype(jnp.float32), value_heads, precision=lax.Precision.HIGHEST)
    return (mixed.astype(jnp.bfloat16).reshape(row_count, -1), attn_probs, probs_half)

def attend_backward(query_rows, key_rows, value_rows, attn_probs, probs_half, grad_mixed, head_count):
    row_count = query_rows.shape[0]
    query_heads = split_heads(query_rows, head_count)
    key_heads = split_heads(key_rows, head_count)
    value_heads = split_heads(value_rows, head_count)
    grad_heads = split_heads(grad_mixed, head_count)
    score_scale = query_heads.shape[2] ** (-0.5)
    grad_probs = jnp.einsum('qhd,khd->hqk', grad_heads, value_heads, precision=lax.Precision.HIGHEST)
    grad_values = jnp.einsum('hqk,qhd->khd', probs_half.astype(jnp.float32), grad_heads, precision=lax.Precision.HIGHEST)
    inner = lax.optimization_barrier(jnp.sum(attn_probs * grad_probs, axis=-1, keepdims=True))
    grad_scores = (attn_probs * (grad_probs - inner)).astype(jnp.bfloat16).astype(jnp.float32)
    grad_queries = jnp.einsum('hqk,khd->qhd', grad_scores, key_heads, precision=lax.Precision.HIGHEST) * score_scale
    grad_keys = jnp.einsum('hqk,qhd->khd', grad_scores, query_heads, precision=lax.Precision.HIGHEST) * score_scale
    pieces_list = [grad_queries, grad_keys, grad_values]
    return jnp.concatenate([p.astype(jnp.bfloat16).reshape(row_count, -1) for p in pieces_list], axis=1)

def reference(tokens, w_qkv, w_out, doc_blocks, cotangent):
    seq_count = doc_blocks.shape[0]
    token_seqs = tokens.reshape(seq_count, TOK_DEV, D)
    grad_seqs = cotangent.reshape(seq_count, TOK_DEV, D)
    head_width = H * HD

    def one_sequence(carry, item):
        seq_rows, seq_grad, doc_ids = item
        allowed = row_mask(doc_ids, TOK_DEV)
        qkv = jnp.dot(seq_rows, w_qkv, preferred_element_type=jnp.float32).astype(jnp.bfloat16)
        query_rows = qkv[:, :head_width]
        key_rows = qkv[:, head_width:2 * head_width]
        value_rows = qkv[:, 2 * head_width:]
        mixed, attn_probs, probs_half = attend_forward(query_rows, key_rows, value_rows, allowed, H)
        output = jnp.dot(mixed, w_out.T, preferred_element_type=jnp.float32).astype(jnp.bfloat16)
        grad_mixed = jnp.dot(seq_grad, w_out, preferred_element_type=jnp.float32).astype(jnp.bfloat16)
        grad_qkv = attend_backward(query_rows, key_rows, value_rows, attn_probs, probs_half, grad_mixed, H)
        grad_tokens = jnp.dot(grad_qkv, w_qkv.T, preferred_element_type=jnp.float32).astype(jnp.bfloat16)
        sum_qkv = carry[0] + jnp.dot(seq_rows.T, grad_qkv, preferred_element_type=jnp.float32)
        sum_out = carry[1] + jnp.dot(seq_grad.T, mixed, preferred_element_type=jnp.float32)
        return ((sum_qkv, sum_out), (output, grad_tokens))
    start_sums = (jnp.zeros((D, 3 * head_width), jnp.float32), jnp.zeros((D, head_width), jnp.float32))
    sums_final, outputs = lax.scan(one_sequence, start_sums, (token_seqs, grad_seqs, doc_blocks))
    norm_factor = 1.0 / math.sqrt(TOKENS)
    output = outputs[0].reshape(TOKENS, D)
    grad_tokens = outputs[1].reshape(TOKENS, D)
    return (output, grad_tokens, sums_final[0] * norm_factor, sums_final[1] * norm_factor)
```

```python
import functools
import math

import jax
import jax.numpy as jnp
from jax import lax
from jax.experimental import pallas as pl
from jax.experimental.pallas import tpu as pltpu
from jax.sharding import PartitionSpec as P

H = 8


NEG_FILL = -1e30
CONTRACT_ROWS = (((0,), (0,)), ((), ()))
CONTRACT_COLS = (((1,), (1,)), ((), ()))


def row_mask(doc_ids, row_count):
    block_len = row_count // doc_ids.shape[0]
    doc_rows = jnp.repeat(doc_ids, block_len, total_repeat_length=row_count)
    position = jnp.arange(row_count, dtype=jnp.int32)
    causal = position[None, :] <= position[:, None]
    return causal & (doc_rows[None, :] == doc_rows[:, None])


def split_heads(matrix, head_count):
    return matrix.reshape(matrix.shape[0], head_count, matrix.shape[1] // head_count)


def attend_forward(query_rows, key_rows, value_rows, allowed, head_count):
    row_count = query_rows.shape[0]
    query_heads = split_heads(query_rows, head_count)
    key_heads = split_heads(key_rows, head_count)
    value_heads = split_heads(value_rows, head_count)
    score_scale = query_heads.shape[2] ** (-0.5)
    scores = (
        jnp.einsum("qhd,khd->hqk", query_heads, key_heads, preferred_element_type=jnp.float32)
        * score_scale
    )
    scores = jnp.where(allowed[None], scores, NEG_FILL)
    highest = jnp.max(scores, axis=-1, keepdims=True)
    expvals = jnp.exp(scores - highest)
    attn_probs = expvals / jnp.sum(expvals, axis=-1, keepdims=True)
    probs_half = attn_probs.astype(jnp.bfloat16)
    mixed = jnp.einsum("hqk,khd->qhd", probs_half, value_heads, preferred_element_type=jnp.float32)
    return (mixed.astype(jnp.bfloat16).reshape(row_count, -1), attn_probs, probs_half)


def attend_backward(
    query_rows, key_rows, value_rows, attn_probs, probs_half, grad_mixed, head_count
):
    row_count = query_rows.shape[0]
    query_heads = split_heads(query_rows, head_count)
    key_heads = split_heads(key_rows, head_count)
    value_heads = split_heads(value_rows, head_count)
    grad_heads = split_heads(grad_mixed, head_count)
    score_scale = query_heads.shape[2] ** (-0.5)
    grad_probs = jnp.einsum(
        "qhd,khd->hqk", grad_heads, value_heads, preferred_element_type=jnp.float32
    )
    grad_values = jnp.einsum(
        "hqk,qhd->khd", probs_half, grad_heads, preferred_element_type=jnp.float32
    )
    inner = jnp.sum(attn_probs * grad_probs, axis=-1, keepdims=True)
    grad_scores = (attn_probs * (grad_probs - inner)).astype(jnp.bfloat16)
    grad_queries = (
        jnp.einsum("hqk,khd->qhd", grad_scores, key_heads, preferred_element_type=jnp.float32)
        * score_scale
    )
    grad_keys = (
        jnp.einsum("hqk,qhd->khd", grad_scores, query_heads, preferred_element_type=jnp.float32)
        * score_scale
    )
    pieces_list = [grad_queries, grad_keys, grad_values]
    return jnp.concatenate(
        [p.astype(jnp.bfloat16).reshape(row_count, -1) for p in pieces_list], axis=1
    )


def body(tokens, w_qkv, w_out, doc_blocks, cotangent):
    row_count = tokens.shape[0]
    head_width = w_out.shape[1]
    head_count = H
    all_devices = lax.axis_size("dp") * lax.axis_size("fsdp")
    allowed = row_mask(doc_blocks[0], row_count)
    columns = tokens
    qkv = jnp.dot(
        columns,
        lax.all_gather(w_qkv, "fsdp", axis=0, tiled=True),
        preferred_element_type=jnp.float32,
    ).astype(jnp.bfloat16)
    query_rows = qkv[:, :head_width]
    key_rows = qkv[:, head_width : 2 * head_width]
    value_rows = qkv[:, 2 * head_width :]
    mixed, attn_probs, probs_half = attend_forward(
        query_rows, key_rows, value_rows, allowed, head_count
    )
    output = lax.dot_general(
        mixed,
        lax.all_gather(w_out, "fsdp", axis=0, tiled=True),
        CONTRACT_COLS,
        preferred_element_type=jnp.float32,
    )
    columns = cotangent
    grad_mixed = jnp.dot(
        columns,
        lax.all_gather(w_out, "fsdp", axis=0, tiled=True),
        preferred_element_type=jnp.float32,
    ).astype(jnp.bfloat16)
    output = output.astype(jnp.bfloat16)
    grad_qkv = attend_backward(
        query_rows, key_rows, value_rows, attn_probs, probs_half, grad_mixed, head_count
    )
    grad_tokens = lax.dot_general(
        grad_qkv,
        lax.all_gather(w_qkv, "fsdp", axis=0, tiled=True),
        CONTRACT_COLS,
        preferred_element_type=jnp.float32,
    )
    grad_tokens = grad_tokens.astype(jnp.bfloat16)
    first_term = lax.dot_general(
        tokens, grad_qkv, CONTRACT_ROWS, preferred_element_type=jnp.float32
    )
    second_term = lax.dot_general(
        cotangent, mixed, CONTRACT_ROWS, preferred_element_type=jnp.float32
    )
    partial_grad = lax.psum_scatter(
        jnp.concatenate([first_term, second_term], axis=1), "fsdp", scatter_dimension=0, tiled=True
    )
    summed = lax.psum(partial_grad, "dp")
    norm_factor = 1.0 / math.sqrt(row_count * all_devices)
    grad_w_qkv = summed[:, : 3 * head_width] * norm_factor
    grad_w_out = summed[:, 3 * head_width :] * norm_factor
    return (output, grad_tokens, grad_w_qkv, grad_w_out)


MESH = pl.DeviceIdType.MESH
HEADS = 4
HD = 128
PLAIN = (((1,), (0,)), ((), ()))


class Place:
    def __init__(self, fsdp_size):
        self.d, self.f = lax.axis_index("dp"), lax.axis_index("fsdp")
        self.c = lax.rem(self.d, 2)
        chip = lax.div(self.d, 2)
        self.x, self.y = lax.rem(chip, 2), lax.div(chip, 2)
        self.dx = self.dp_of(self.y, 1 - self.x, self.c)
        self.dy = self.dp_of(1 - self.y, self.x, self.c)
        self.dc = self.dp_of(self.y, self.x, 1 - self.c)
        self.q = self.y * 2 + self.x
        self.qx = self.y * 2 + 1 - self.x
        self.qy = (1 - self.y) * 2 + self.x
        self.n = fsdp_size

    def dp_of(self, y, x, c):
        return (y * 2 + x) * 2 + c

    def ahead(self, j):
        return lax.rem(self.f + j, self.n)

    def behind(self, j):
        return lax.rem(self.f + self.n - j, self.n)

    def barrier(self):
        sem = pltpu.get_barrier_semaphore()
        targets = [(self.dx, self.f), (self.dy, self.f), (self.dc, self.f)]
        targets += [(self.d, self.ahead(j)) for j in range(1, self.n)]
        for target in targets:
            pl.semaphore_signal(sem, inc=1, device_id=target, device_id_type=MESH)
        pl.semaphore_wait(sem, len(targets))


def dot(left, right, dims=PLAIN):
    return lax.dot_general(left, right, dims, preferred_element_type=jnp.float32)


def remote(src, dst, send_sem, recv_sem, target):
    return pltpu.make_async_remote_copy(
        src_ref=src,
        dst_ref=dst,
        send_sem=send_sem,
        recv_sem=recv_sem,
        device_id=target,
        device_id_type=MESH,
    )


def loop(count, work):
    def step(i, carry):
        work(i)
        return carry

    lax.fori_loop(0, count, step, 0)


def layer_kernel(
    n,
    tok_ref,
    cot_ref,
    wq_ref,
    wo_ref,
    doc_ref,
    sum_ref,
    out_ref,
    gt_ref,
    toks,
    cots,
    toks_t,
    cots_t,
    bias,
    w,
    x,
    g,
    grads,
    pair,
    plane,
    z_terms,
    part_out,
    part_in,
    g_send,
    g_recv,
    r_send,
    r_recv,
    c_send,
    c_recv,
    local_sem,
):
    me = Place(n)
    rows = toks.shape[1]
    wide = toks.shape[2]
    shard = wide // n
    quarter = shard // 4
    half = quarter // 2
    sub = 2 * HD
    last = HEADS - 1
    scale = HD ** (-0.5)

    def load_act(i):
        src, dst = ((tok_ref, toks), (cot_ref, cots))[i]
        return pltpu.make_async_copy(src, dst.at[0], local_sem.at[i])

    def load_w(k, p):
        src, base = (wq_ref, p * wo_ref.shape[1]) if p < 3 else (wo_ref, 0)
        first = pl.multiple_of(base + (me.c * HEADS + k) * HD, HD)
        spot = pl.ds(pl.multiple_of(me.f * shard, shard), shard)
        return pltpu.make_async_copy(
            src.at[:, pl.ds(first, HD)],
            w.at[k, spot, pl.ds(p * HD, HD)],
            local_sem.at[2 + k * 4 + p],
        )

    for k in range(HEADS):
        for p in range(4):
            load_w(k, p).start()
        if k < 2:
            load_act(k).start()
    me.barrier()

    def span(k, f, q, first, count):
        start = pl.multiple_of(f * shard + q * quarter + first, half)
        return w.at[k, pl.ds(start, count)]

    def gather(kind, k, j):
        f = me.f if kind == 0 else me.behind(j)
        q, first, count, target = (
            (me.q, 0, quarter, (me.d, me.ahead(j))),
            (me.q, 0, quarter, (me.dx, me.f)),
            (me.q, 0, quarter, (me.dy, me.f)),
            (me.qx, 0, half, (me.dy, me.f)),
            (me.qy, half, half, (me.dx, me.f)),
        )[kind]
        spot = span(k, f, q, first, count)
        slot = kind * (n - 1) + j - 1
        return remote(spot, spot, g_send.at[k, slot], g_recv.at[k, slot], target)

    for k in range(HEADS):
        for p in range(4):
            load_w(k, p).wait()
        for j in range(1, n):
            gather(0, k, j).start()

    def relay_z(k):
        for j in range(1, n):
            gather(0, k, j).wait_recv()
            gather(1, k, j).start()
            gather(2, k, j).start()

    def relay_plane(k):
        for j in range(1, n):
            gather(1, k, j).wait_recv()
            gather(3, k, j).start()
            gather(2, k, j).wait_recv()
            gather(4, k, j).start()

    def gathered(k):
        for j in range(1, n):
            gather(3, k, j).wait_recv()
            gather(4, k, j).wait_recv()

    def cross(i):
        src, dst = (
            (toks.at[0], toks.at[1]),
            (cots.at[0], cots.at[1]),
            (bias.at[0], bias.at[1]),
            (part_out.at[0], part_in.at[0]),
            (part_out.at[1], part_in.at[1]),
        )[i]
        return remote(src, dst, c_send.at[i], c_recv.at[i], (me.dc, me.f))

    for i in range(2):
        load_act(i).wait()
        cross(i).start()

    block = rows // doc_ref.shape[1]
    key_row = lax.broadcasted_iota(jnp.int32, (rows, rows), 0)
    query_row = lax.broadcasted_iota(jnp.int32, (rows, rows), 1)

    def doc_of(row):
        ids = jnp.full(row.shape, doc_ref[0, 0], jnp.int32)
        for b in range(1, doc_ref.shape[1]):
            ids = jnp.where(row >= b * block, doc_ref[0, b], ids)
        return ids

    docs_k = doc_of(lax.broadcasted_iota(jnp.int32, (rows, HD), 0))
    docs_q = doc_of(lax.broadcasted_iota(jnp.int32, (8, rows), 1))
    same = docs_k[:, :1] == docs_q[:1, :]
    allowed = same & (key_row <= query_row)
    bias[0] = jnp.where(allowed, 0.0, NEG_FILL).astype(jnp.bfloat16)
    cross(2).start()

    def turn(s):
        def one(i):
            part = pl.ds(pl.multiple_of(i * HD, HD), HD)
            spot = pl.ds(s * rows, rows)
            toks_t[part, spot] = toks[s, :, part].T
            cots_t[part, spot] = cots[s, :, part].T

        loop(wide // HD, one)

    turn(0)
    relay_z(0)
    for i in range(2):
        cross(i).wait_recv()
    turn(1)
    relay_plane(0)
    cross(2).wait_recv()

    def project(k):
        def one(i):
            s, r = lax.div(i, 2), lax.rem(i, 2)
            spot = pl.ds(pl.multiple_of(r * (rows // 2), rows // 2), rows // 2)
            x[s, spot, : 3 * HD] = dot(toks[s, spot, :], w[k, :, : 3 * HD]).astype(jnp.bfloat16)
            x[s, spot, 3 * HD :] = dot(cots[s, spot, :], w[k, :, 3 * HD :]).astype(jnp.bfloat16)

        loop(4, one)

    def attend(k, s):
        key, value = x[s, :, HD : 2 * HD], x[s, :, 2 * HD : 3 * HD]
        key_t, value_t = key.T, value.T
        grad_k, grad_v = None, None
        base = pl.multiple_of(s * rows, rows)
        for part in (1, 0):
            span_q = slice(part * rows // 2, (part + 1) * rows // 2)
            deep = (part + 1) * rows // 2
            query, gm = x[s, span_q, :HD], x[s, span_q, 3 * HD :]
            scores = dot(key[:deep], query, CONTRACT_COLS) * scale
            scores = scores + bias[s, :deep, span_q].astype(jnp.float32)
            expvals = jnp.exp(scores - jnp.max(scores, axis=0, keepdims=True))
            probs = expvals / jnp.sum(expvals, axis=0, keepdims=True)
            probs_half = probs.astype(jnp.bfloat16)
            mixed = dot(value_t[:, :deep], probs_half).astype(jnp.bfloat16)
            grad_probs = dot(value[:deep], gm, CONTRACT_COLS)
            inner = jnp.sum(probs * grad_probs, axis=0, keepdims=True)
            grad_scores = (probs * (grad_probs - inner)).astype(jnp.bfloat16)
            grad_q = (dot(key_t[:, :deep], grad_scores) * scale).astype(jnp.bfloat16)
            spot = pl.ds(base + part * (rows // 2), rows // 2)
            g[k, spot, :HD] = grad_q.T
            g[k, spot, 3 * HD :] = mixed.T
            more_k, more_v = dot(grad_scores, query), dot(probs_half, gm)
            if part == 1:
                grad_k, grad_v = more_k, more_v
            else:
                low = pl.ds(base, rows // 2)
                high = pl.ds(base + rows // 2, rows // 2)
                more_k, more_v = more_k + grad_k[:deep], more_v + grad_v[:deep]
                g[k, low, HD : 2 * HD] = (more_k * scale).astype(jnp.bfloat16)
                g[k, low, 2 * HD : 3 * HD] = more_v.astype(jnp.bfloat16)
                g[k, high, HD : 2 * HD] = (grad_k[deep:] * scale).astype(jnp.bfloat16)
                g[k, high, 2 * HD : 3 * HD] = grad_v[deep:].astype(jnp.bfloat16)

    def weight_grad(k, a):
        m = 2 * k + a

        def one(f):
            spot = pl.ds(pl.multiple_of(f * shard, shard), shard)
            if a == 0:
                total = dot(toks_t[spot, :], g[k, :, :sub]).astype(jnp.bfloat16)
                grads[m, f] = total.reshape(2, 2, quarter, sub)
            else:
                left = dot(toks_t[spot, :], g[k, :, sub : 3 * HD]).astype(jnp.bfloat16)
                right = dot(cots_t[spot, :], g[k, :, 3 * HD :]).astype(jnp.bfloat16)
                grads[m, f, :, :, :, :HD] = left.reshape(2, 2, quarter, HD)
                grads[m, f, :, :, :, HD:] = right.reshape(2, 2, quarter, HD)

        loop(n, one)

    def reduce(kind, k, a, j=0):
        m = 2 * k + a
        over_x, over_y = (me.dx, me.f), (me.dy, me.f)
        mine = sum_ref.at[me.c, m, me.q]
        from_x, from_y = sum_ref.at[me.c, m, me.qx], sum_ref.at[me.c, m, me.qy]
        if kind == 0:
            src = grads.at[m, :, :, 1 - me.x] if a == 0 else grads.at[m, :, 1 - me.y]
            dst, target = pair.at[m], over_x if a == 0 else over_y
        elif kind == 1:
            src = pair.at[m, :, 1 - me.y] if a == 0 else pair.at[m, :, 1 - me.x]
            dst, target = plane.at[m], over_y if a == 0 else over_x
        elif kind == 2:
            src, dst = plane.at[m, me.ahead(j)], z_terms.at[m, j - 1]
            target = (me.d, me.ahead(j))
        elif kind == 3:
            src, dst, target = mine, mine, over_x
        elif kind == 4:
            src, dst, target = mine, mine, over_y
        elif kind == 5:
            src = from_x.at[pl.ds(0, half)]
            dst, target = src, over_y
        elif kind == 6:
            src = from_y.at[pl.ds(half, half)]
            dst, target = src, over_x
        else:
            src = sum_ref.at[me.c, m]
            dst, target = src, (me.dc, me.f)
        slot = kind if kind != 2 else 7 + j
        return remote(src, dst, r_send.at[m, slot], r_recv.at[m, slot], target)

    def add(left, right):
        return (left.astype(jnp.float32) + right.astype(jnp.float32)).astype(jnp.bfloat16)

    def stage_pair(k, a):
        m = 2 * k + a
        reduce(0, k, a).wait_recv()

        def one(i):
            f, other = lax.div(i, 2), lax.rem(i, 2)
            own = grads[m, f, other, me.x] if a == 0 else grads[m, f, me.y, other]
            pair[m, f, other] = add(own, pair[m, f, other])

        loop(2 * n, one)
        reduce(1, k, a).start()

    def stage_plane(k, a):
        m = 2 * k + a
        reduce(1, k, a).wait_recv()
        keep = me.y if a == 0 else me.x

        def one(f):
            plane[m, f] = add(pair[m, f, keep], plane[m, f])

        loop(n, one)
        for j in range(1, n):
            reduce(2, k, a, j).start()

    def stage_z(k, a):
        m = 2 * k + a
        total = plane[m, me.f].astype(jnp.float32)
        for j in range(1, n):
            reduce(2, k, a, j).wait_recv()
            total = total + z_terms[m, j - 1].astype(jnp.float32)
        sum_ref[me.c, m, me.q] = total.astype(jnp.bfloat16)
        reduce(3, k, a).start()
        reduce(4, k, a).start()

    def stage_spread(k, a):
        reduce(3, k, a).wait_recv()
        reduce(5, k, a).start()
        reduce(4, k, a).wait_recv()
        reduce(6, k, a).start()

    def stage_last(k, a):
        reduce(5, k, a).wait_recv()
        reduce(6, k, a).wait_recv()
        reduce(7, k, a).start()

    def both(stage, k):
        stage(k, 0)
        stage(k, 1)

    def head(k):
        gathered(k)
        project(k)

        @pl.when(k < last)
        def _():
            relay_z(k + 1)

        def sequence(s):
            attend(k, s)

            @pl.when((s == 0) & (k < last))
            def _():
                relay_plane(k + 1)

            @pl.when((s == 0) & (k > 0))
            def _():
                both(stage_pair, k - 1)

        loop(2, sequence)

        @pl.when(k > 0)
        def _():
            both(stage_plane, k - 1)

        for a in range(2):
            weight_grad(k, a)
            reduce(0, k, a).start()

        @pl.when(k > 0)
        def _():
            both(stage_z, k - 1)

    loop(HEADS, head)

    def product(which, s, i):
        cols = pl.ds(pl.multiple_of(i * sub, sub), sub)
        spot = pl.ds(s * rows, rows)
        part = slice(3 * HD, 4 * HD) if which == 0 else slice(0, 3 * HD)
        total = None
        for k in range(HEADS):
            more = dot(g[k, spot, part], w[k, cols, part], CONTRACT_COLS)
            total = more if total is None else total + more
        if s == 1:
            part_out[which, :, cols] = total.astype(jnp.bfloat16)
        else:
            total = total + part_in[which, :, cols].astype(jnp.float32)
            target = (out_ref, gt_ref)[which]
            target[:, cols] = total.astype(jnp.bfloat16)

    def products(which, s):
        loop(wide // sub, functools.partial(product, which, s))

    products(0, 1)
    cross(3).start()
    both(stage_pair, last)
    both(stage_spread, 0)
    products(1, 1)
    cross(4).start()
    both(stage_spread, 1)
    both(stage_spread, 2)
    both(stage_plane, last)
    cross(3).wait_recv()
    products(0, 0)
    both(stage_last, 0)
    both(stage_last, 1)
    both(stage_z, last)
    cross(4).wait_recv()
    products(1, 0)
    both(stage_spread, last)
    both(stage_last, 2)
    both(stage_last, last)

    def drain(k):
        for kind in range(5):
            for j in range(1, n):
                gather(kind, k, j).wait_send()
        for a in range(2):
            for kind in (0, 1, 3, 4, 5, 6, 7):
                reduce(kind, k, a).wait_send()
            for j in range(1, n):
                reduce(2, k, a, j).wait_send()
            reduce(7, k, a).wait_recv()

    loop(HEADS, drain)
    for i in range(5):
        cross(i).wait_send()


def layer(n, tokens, cotangent, w_qkv, w_out, doc_blocks):
    rows, wide = tokens.shape
    shard = wide // n
    quarter = shard // 4
    subs = 2 * HEADS
    vmem = pl.BlockSpec(memory_space=pltpu.VMEM)
    anywhere = pl.BlockSpec(memory_space=pl.ANY)

    def room(*shape):
        return pltpu.VMEM(shape, jnp.bfloat16)

    dma = pltpu.SemaphoreType.DMA
    return pl.pallas_call(
        functools.partial(layer_kernel, n),
        out_shape=[
            jax.ShapeDtypeStruct((2, subs, 4, quarter, 2 * HD), jnp.bfloat16),
            jax.ShapeDtypeStruct((rows, wide), jnp.bfloat16),
            jax.ShapeDtypeStruct((rows, wide), jnp.bfloat16),
        ],
        in_specs=[anywhere] * 4 + [pl.BlockSpec(memory_space=pltpu.SMEM)],
        out_specs=[vmem] * 3,
        scratch_shapes=[
            room(2, rows, wide),
            room(2, rows, wide),
            room(wide, 2 * rows),
            room(wide, 2 * rows),
            room(2, rows, rows),
            room(HEADS, wide, 4 * HD),
            room(2, rows, 4 * HD),
            room(HEADS, 2 * rows, 4 * HD),
            room(subs, n, 2, 2, quarter, 2 * HD),
            room(subs, n, 2, quarter, 2 * HD),
            room(subs, n, quarter, 2 * HD),
            room(subs, n - 1, quarter, 2 * HD),
            room(2, rows, wide),
            room(2, rows, wide),
            dma((HEADS, 5 * (n - 1))),
            dma((HEADS, 5 * (n - 1))),
            dma((subs, 7 + n)),
            dma((subs, 7 + n)),
            dma((5,)),
            dma((5,)),
            dma((2 + 4 * HEADS,)),
        ],
        compiler_params=pltpu.CompilerParams(
            collective_id=0, has_side_effects=True, vmem_limit_bytes=56 << 20
        ),
        name="layer",
    )(tokens, cotangent, w_qkv, w_out, doc_blocks)


def finish_kernel(norm, sum_ref, out_in, gt_in, out_ref, gt_ref, gq_ref, go_ref):
    out_ref[...] = out_in[...]
    gt_ref[...] = gt_in[...]
    width = go_ref.shape[1]
    for c in range(2):
        for m in range(2 * HEADS):
            head = c * HEADS + m // 2
            for i in range(2):
                value = sum_ref[c, m, 0, :, i * HD : (i + 1) * HD].astype(jnp.float32) * norm
                p = (m % 2) * 2 + i
                if p < 3:
                    gq_ref[:, p * width + head * HD : p * width + (head + 1) * HD] = value
                else:
                    go_ref[:, head * HD : (head + 1) * HD] = value


def finish(norm, sums, output, grad_tokens):
    rows, wide = output.shape
    quarter, width = sums.shape[3], 2 * HEADS * HD
    act = pl.BlockSpec((rows // 4, wide), lambda q: (q, 0))
    return pl.pallas_call(
        functools.partial(finish_kernel, norm),
        grid=(4,),
        out_shape=[
            jax.ShapeDtypeStruct((rows, wide), jnp.bfloat16),
            jax.ShapeDtypeStruct((rows, wide), jnp.bfloat16),
            jax.ShapeDtypeStruct((4 * quarter, 3 * width), jnp.float32),
            jax.ShapeDtypeStruct((4 * quarter, width), jnp.float32),
        ],
        in_specs=[
            pl.BlockSpec((2, 2 * HEADS, 1, quarter, 2 * HD), lambda q: (0, 0, q, 0, 0)),
            act,
            act,
        ],
        out_specs=[
            act,
            act,
            pl.BlockSpec((quarter, 3 * width), lambda q: (q, 0)),
            pl.BlockSpec((quarter, width), lambda q: (q, 0)),
        ],
        compiler_params=pltpu.CompilerParams(vmem_limit_bytes=32 << 20),
        name="finish",
    )(sums, output, grad_tokens)


def chip_body(tokens, w_qkv, w_out, doc_blocks, cotangent):
    n = lax.axis_size("fsdp")
    all_devices = lax.axis_size("dp") * n
    sums, output, grad_tokens = layer(n, tokens, cotangent, w_qkv, w_out, doc_blocks)
    norm_factor = 1.0 / math.sqrt(tokens.shape[0] * all_devices)
    return tuple(finish(norm_factor, sums, output, grad_tokens))


def solution(mesh):
    placed = (
        P(("dp", "fsdp"), None),
        P("fsdp", None),
        P("fsdp", None),
        P(("dp", "fsdp"), None),
        P(("dp", "fsdp"), None),
    )
    in_plane = mesh.shape["dp"] == 8 and mesh.shape["fsdp"] == 4
    return jax.shard_map(
        chip_body if in_plane else body,
        mesh=mesh,
        in_specs=placed,
        out_specs=(
            P(("dp", "fsdp"), None),
            P(("dp", "fsdp"), None),
            P("fsdp", None),
            P("fsdp", None),
        ),
        check_vma=False,
    )
```

```python
import functools
import math

import jax
import jax.numpy as jnp
from jax import lax
from jax.experimental import pallas as pl
from jax.experimental.pallas import tpu as pltpu
from jax.sharding import PartitionSpec as P

H = 8


NEG_FILL = -1e30
CONTRACT_ROWS = (((0,), (0,)), ((), ()))
CONTRACT_COLS = (((1,), (1,)), ((), ()))


def row_mask(doc_ids, row_count):
    block_len = row_count // doc_ids.shape[0]
    doc_rows = jnp.repeat(doc_ids, block_len, total_repeat_length=row_count)
    position = jnp.arange(row_count, dtype=jnp.int32)
    causal = position[None, :] <= position[:, None]
    return causal & (doc_rows[None, :] == doc_rows[:, None])


def split_heads(matrix, head_count):
    return matrix.reshape(matrix.shape[0], head_count, matrix.shape[1] // head_count)


def attend_forward(query_rows, key_rows, value_rows, allowed, head_count):
    row_count = query_rows.shape[0]
    query_heads = split_heads(query_rows, head_count)
    key_heads = split_heads(key_rows, head_count)
    value_heads = split_heads(value_rows, head_count)
    score_scale = query_heads.shape[2] ** (-0.5)
    scores = (
        jnp.einsum("qhd,khd->hqk", query_heads, key_heads, preferred_element_type=jnp.float32)
        * score_scale
    )
    scores = jnp.where(allowed[None], scores, NEG_FILL)
    highest = jnp.max(scores, axis=-1, keepdims=True)
    expvals = jnp.exp(scores - highest)
    attn_probs = expvals / jnp.sum(expvals, axis=-1, keepdims=True)
    probs_half = attn_probs.astype(jnp.bfloat16)
    mixed = jnp.einsum("hqk,khd->qhd", probs_half, value_heads, preferred_element_type=jnp.float32)
    return (mixed.astype(jnp.bfloat16).reshape(row_count, -1), attn_probs, probs_half)


def attend_backward(
    query_rows, key_rows, value_rows, attn_probs, probs_half, grad_mixed, head_count
):
    row_count = query_rows.shape[0]
    query_heads = split_heads(query_rows, head_count)
    key_heads = split_heads(key_rows, head_count)
    value_heads = split_heads(value_rows, head_count)
    grad_heads = split_heads(grad_mixed, head_count)
    score_scale = query_heads.shape[2] ** (-0.5)
    grad_probs = jnp.einsum(
        "qhd,khd->hqk", grad_heads, value_heads, preferred_element_type=jnp.float32
    )
    grad_values = jnp.einsum(
        "hqk,qhd->khd", probs_half, grad_heads, preferred_element_type=jnp.float32
    )
    inner = jnp.sum(attn_probs * grad_probs, axis=-1, keepdims=True)
    grad_scores = (attn_probs * (grad_probs - inner)).astype(jnp.bfloat16)
    grad_queries = (
        jnp.einsum("hqk,khd->qhd", grad_scores, key_heads, preferred_element_type=jnp.float32)
        * score_scale
    )
    grad_keys = (
        jnp.einsum("hqk,qhd->khd", grad_scores, query_heads, preferred_element_type=jnp.float32)
        * score_scale
    )
    pieces_list = [grad_queries, grad_keys, grad_values]
    return jnp.concatenate(
        [p.astype(jnp.bfloat16).reshape(row_count, -1) for p in pieces_list], axis=1
    )


def body(tokens, w_qkv, w_out, doc_blocks, cotangent):
    row_count = tokens.shape[0]
    head_width = w_out.shape[1]
    head_count = H
    all_devices = lax.axis_size("dp") * lax.axis_size("fsdp")
    allowed = row_mask(doc_blocks[0], row_count)
    columns = tokens
    qkv = jnp.dot(
        columns,
        lax.all_gather(w_qkv, "fsdp", axis=0, tiled=True),
        preferred_element_type=jnp.float32,
    ).astype(jnp.bfloat16)
    query_rows = qkv[:, :head_width]
    key_rows = qkv[:, head_width : 2 * head_width]
    value_rows = qkv[:, 2 * head_width :]
    mixed, attn_probs, probs_half = attend_forward(
        query_rows, key_rows, value_rows, allowed, head_count
    )
    output = lax.dot_general(
        mixed,
        lax.all_gather(w_out, "fsdp", axis=0, tiled=True),
        CONTRACT_COLS,
        preferred_element_type=jnp.float32,
    )
    columns = cotangent
    grad_mixed = jnp.dot(
        columns,
        lax.all_gather(w_out, "fsdp", axis=0, tiled=True),
        preferred_element_type=jnp.float32,
    ).astype(jnp.bfloat16)
    output = output.astype(jnp.bfloat16)
    grad_qkv = attend_backward(
        query_rows, key_rows, value_rows, attn_probs, probs_half, grad_mixed, head_count
    )
    grad_tokens = lax.dot_general(
        grad_qkv,
        lax.all_gather(w_qkv, "fsdp", axis=0, tiled=True),
        CONTRACT_COLS,
        preferred_element_type=jnp.float32,
    )
    grad_tokens = grad_tokens.astype(jnp.bfloat16)
    first_term = lax.dot_general(
        tokens, grad_qkv, CONTRACT_ROWS, preferred_element_type=jnp.float32
    )
    second_term = lax.dot_general(
        cotangent, mixed, CONTRACT_ROWS, preferred_element_type=jnp.float32
    )
    partial_grad = lax.psum_scatter(
        jnp.concatenate([first_term, second_term], axis=1), "fsdp", scatter_dimension=0, tiled=True
    )
    summed = lax.psum(partial_grad, "dp")
    norm_factor = 1.0 / math.sqrt(row_count * all_devices)
    grad_w_qkv = summed[:, : 3 * head_width] * norm_factor
    grad_w_out = summed[:, 3 * head_width :] * norm_factor
    return (output, grad_tokens, grad_w_qkv, grad_w_out)


MESH = pl.DeviceIdType.MESH
HEADS = 4
HD = 128
PLAIN = (((1,), (0,)), ((), ()))


class Place:
    def __init__(self, fsdp_size):
        self.d, self.f = lax.axis_index("dp"), lax.axis_index("fsdp")
        self.c = lax.rem(self.d, 2)
        chip = lax.div(self.d, 2)
        self.x, self.y = lax.rem(chip, 2), lax.div(chip, 2)
        self.dx = self.dp_of(self.y, 1 - self.x, self.c)
        self.dy = self.dp_of(1 - self.y, self.x, self.c)
        self.dc = self.dp_of(self.y, self.x, 1 - self.c)
        self.q = self.y * 2 + self.x
        self.qx = self.y * 2 + 1 - self.x
        self.qy = (1 - self.y) * 2 + self.x
        self.n = fsdp_size

    def dp_of(self, y, x, c):
        return (y * 2 + x) * 2 + c

    def ahead(self, j):
        return lax.rem(self.f + j, self.n)

    def behind(self, j):
        return lax.rem(self.f + self.n - j, self.n)

    def barrier(self):
        sem = pltpu.get_barrier_semaphore()
        targets = [(self.dx, self.f), (self.dy, self.f), (self.dc, self.f)]
        targets += [(self.d, self.ahead(j)) for j in range(1, self.n)]
        for target in targets:
            pl.semaphore_signal(sem, inc=1, device_id=target, device_id_type=MESH)
        pl.semaphore_wait(sem, len(targets))


def dot(left, right, dims=PLAIN):
    return lax.dot_general(left, right, dims, preferred_element_type=jnp.float32)


def remote(src, dst, send_sem, recv_sem, target):
    return pltpu.make_async_remote_copy(
        src_ref=src,
        dst_ref=dst,
        send_sem=send_sem,
        recv_sem=recv_sem,
        device_id=target,
        device_id_type=MESH,
    )


def loop(count, work):
    def step(i, carry):
        work(i)
        return carry

    lax.fori_loop(0, count, step, 0)


def layer_kernel(
    n,
    tok_ref,
    cot_ref,
    wq_ref,
    wo_ref,
    doc_ref,
    sum_ref,
    out_ref,
    gt_ref,
    toks,
    cots,
    toks_t,
    cots_t,
    bias,
    w,
    x,
    g,
    grads,
    pair,
    plane,
    z_terms,
    part_out,
    part_in,
    result,
    sums,
    z_first,
    z_sum,
    pair_first,
    plane_first,
    g_send,
    g_recv,
    r_send,
    r_recv,
    c_send,
    c_recv,
    local_sem,
):
    me = Place(n)
    rows = toks.shape[1]
    wide = toks.shape[2]
    shard = wide // n
    quarter = shard // 4
    half = quarter // 2
    sub = 2 * HD
    last = HEADS - 1
    scale = HD ** (-0.5)

    def load_act(i):
        src, dst = ((tok_ref, toks), (cot_ref, cots))[i]
        return pltpu.make_async_copy(src, dst.at[0], local_sem.at[i])

    def load_w(k, p):
        src, base = (wq_ref, p * wo_ref.shape[1]) if p < 3 else (wo_ref, 0)
        first = pl.multiple_of(base + (me.c * HEADS + k) * HD, HD)
        spot = pl.ds(pl.multiple_of(me.f * shard, shard), shard)
        return pltpu.make_async_copy(
            src.at[:, pl.ds(first, HD)],
            w.at[k, spot, pl.ds(p * HD, HD)],
            local_sem.at[2 + k * 4 + p],
        )

    for k in range(HEADS):
        for p in range(4):
            load_w(k, p).start()
        if k < 2:
            load_act(k).start()
    me.barrier()

    def span(k, f, q, first, count):
        start = pl.multiple_of(f * shard + q * quarter + first, half)
        return w.at[k, pl.ds(start, count)]

    def gather(kind, k, j):
        f = me.f if kind == 0 else me.behind(j)
        q, first, count, target = (
            (me.q, 0, quarter, (me.d, me.ahead(j))),
            (me.q, 0, quarter, (me.dx, me.f)),
            (me.q, 0, quarter, (me.dy, me.f)),
            (me.qx, 0, half, (me.dy, me.f)),
            (me.qy, half, half, (me.dx, me.f)),
        )[kind]
        spot = span(k, f, q, first, count)
        slot = kind * (n - 1) + j - 1
        return remote(spot, spot, g_send.at[k, slot], g_recv.at[k, slot], target)

    for k in range(HEADS):
        for p in range(4):
            load_w(k, p).wait()
        for j in range(1, n):
            gather(0, k, j).start()

    def relay_z(k):
        for j in range(1, n):
            gather(0, k, j).wait_recv()
            gather(1, k, j).start()
            gather(2, k, j).start()

    def relay_plane(k):
        for j in range(1, n):
            gather(1, k, j).wait_recv()
            gather(3, k, j).start()
            gather(2, k, j).wait_recv()
            gather(4, k, j).start()

    def gathered(k):
        for j in range(1, n):
            gather(3, k, j).wait_recv()
            gather(4, k, j).wait_recv()

    def cross(i):
        src, dst = (
            (toks.at[0], toks.at[1]),
            (cots.at[0], cots.at[1]),
            (bias.at[0], bias.at[1]),
            (part_out.at[0], part_in.at[0]),
            (part_out.at[1], part_in.at[1]),
        )[i]
        return remote(src, dst, c_send.at[i], c_recv.at[i], (me.dc, me.f))

    for i in range(2):
        load_act(i).wait()
        cross(i).start()

    block = rows // doc_ref.shape[1]
    key_row = lax.broadcasted_iota(jnp.int32, (rows, rows), 0)
    query_row = lax.broadcasted_iota(jnp.int32, (rows, rows), 1)

    def doc_of(row):
        ids = jnp.full(row.shape, doc_ref[0, 0], jnp.int32)
        for b in range(1, doc_ref.shape[1]):
            ids = jnp.where(row >= b * block, doc_ref[0, b], ids)
        return ids

    docs_k = doc_of(lax.broadcasted_iota(jnp.int32, (rows, HD), 0))
    docs_q = doc_of(lax.broadcasted_iota(jnp.int32, (8, rows), 1))
    same = docs_k[:, :1] == docs_q[:1, :]
    allowed = same & (key_row <= query_row)
    bias[0] = jnp.where(allowed, 0.0, NEG_FILL).astype(jnp.bfloat16)
    cross(2).start()

    def turn(s):
        def one(i):
            part = pl.ds(pl.multiple_of(i * HD, HD), HD)
            spot = pl.ds(s * rows, rows)
            toks_t[part, spot] = toks[s, :, part].T
            cots_t[part, spot] = cots[s, :, part].T

        loop(wide // HD, one)

    turn(0)
    relay_z(0)
    for i in range(2):
        cross(i).wait_recv()
    turn(1)
    relay_plane(0)
    relay_z(1)
    cross(2).wait_recv()

    def project(k):
        def one(s):
            x[s, :, : 3 * HD] = dot(toks[s], w[k, :, : 3 * HD]).astype(jnp.bfloat16)
            x[s, :, 3 * HD :] = dot(cots[s], w[k, :, 3 * HD :]).astype(jnp.bfloat16)

        loop(2, one)

    def attend(k, s):
        key, value = x[s, :, HD : 2 * HD], x[s, :, 2 * HD : 3 * HD]
        key_t, value_t = key.T, value.T
        grad_k, grad_v = None, None
        base = pl.multiple_of(s * rows, rows)
        for part in (1, 0):
            span_q = slice(part * rows // 2, (part + 1) * rows // 2)
            deep = (part + 1) * rows // 2
            query, gm = x[s, span_q, :HD], x[s, span_q, 3 * HD :]
            scores = dot(key[:deep], query, CONTRACT_COLS) * scale
            scores = scores + bias[s, :deep, span_q].astype(jnp.float32)
            expvals = jnp.exp(scores - jnp.max(scores, axis=0, keepdims=True))
            probs = expvals * (1.0 / jnp.sum(expvals, axis=0, keepdims=True))
            probs_half = probs.astype(jnp.bfloat16)
            mixed = dot(value_t[:, :deep], probs_half).astype(jnp.bfloat16)
            grad_probs = dot(value[:deep], gm, CONTRACT_COLS)
            inner = jnp.sum(probs * grad_probs, axis=0, keepdims=True)
            grad_scores = (probs * (grad_probs - inner)).astype(jnp.bfloat16)
            grad_q = (dot(key_t[:, :deep], grad_scores) * scale).astype(jnp.bfloat16)
            spot = pl.ds(base + part * (rows // 2), rows // 2)
            g[k, spot, :HD] = grad_q.T
            g[k, spot, 3 * HD :] = mixed.T
            more_k, more_v = dot(grad_scores, query), dot(probs_half, gm)
            if part == 1:
                grad_k, grad_v = more_k, more_v
            else:
                low = pl.ds(base, rows // 2)
                high = pl.ds(base + rows // 2, rows // 2)
                more_k, more_v = more_k + grad_k[:deep], more_v + grad_v[:deep]
                g[k, low, HD : 2 * HD] = (more_k * scale).astype(jnp.bfloat16)
                g[k, low, 2 * HD : 3 * HD] = more_v.astype(jnp.bfloat16)
                g[k, high, HD : 2 * HD] = (grad_k[deep:] * scale).astype(jnp.bfloat16)
                g[k, high, 2 * HD : 3 * HD] = grad_v[deep:].astype(jnp.bfloat16)

    def weight_grad(k, a):
        m = 2 * k + a

        def one(i):
            deep = 2 * shard
            spot = pl.ds(pl.multiple_of(i * deep, deep), deep)
            fs = pl.ds(2 * i, 2)
            if a == 0:
                total = dot(toks_t[spot, :], g[k, :, :sub]).astype(jnp.bfloat16)
                grads[m, fs] = total.reshape(2, 2, 2, quarter, sub)
            else:
                left = dot(toks_t[spot, :], g[k, :, sub : 3 * HD]).astype(jnp.bfloat16)
                right = dot(cots_t[spot, :], g[k, :, 3 * HD :]).astype(jnp.bfloat16)
                grads[m, fs, :, :, :, :HD] = left.reshape(2, 2, 2, quarter, HD)
                grads[m, fs, :, :, :, HD:] = right.reshape(2, 2, 2, quarter, HD)

        loop(n // 2, one)

    def reduce(kind, k, a, j=0):
        m = 2 * k + a
        over_x, over_y = (me.dx, me.f), (me.dy, me.f)
        mine = sums.at[m, me.q]
        from_x, from_y = sums.at[m, me.qx], sums.at[m, me.qy]
        if kind == 0:
            src = grads.at[m, :, :, 1 - me.x] if a == 0 else grads.at[m, :, 1 - me.y]
            dst, target = pair.at[m], over_x if a == 0 else over_y
        elif kind == 1:
            src = pair.at[m, :, 1 - me.y] if a == 0 else pair.at[m, :, 1 - me.x]
            dst, target = plane.at[m], over_y if a == 0 else over_x
        elif kind == 2:
            src, dst = plane.at[m, me.ahead(j)], z_terms.at[m, j - 1]
            target = (me.d, me.ahead(j))
        elif kind == 3:
            src, dst, target = mine, mine, over_x
        elif kind == 4:
            src, dst, target = mine, mine, over_y
        elif kind == 5:
            src = from_x.at[pl.ds(0, half)]
            dst, target = src, over_y
        elif kind == 6:
            src = from_y.at[pl.ds(half, half)]
            dst, target = src, over_x
        else:
            src, dst, target = sums.at[m], sum_ref.at[me.c, m], (me.dc, me.f)
        slot = kind if kind != 2 else 7 + j
        return remote(src, dst, r_send.at[m, slot], r_recv.at[m, slot], target)

    def first(kind, a, j=0):
        over_x, over_y = (me.dx, me.f), (me.dy, me.f)
        if kind == 0:
            src = z_sum.at[a, :, 1 - me.x] if a == 0 else z_sum.at[a, 1 - me.y]
            dst, target = pair_first.at[a], over_x if a == 0 else over_y
        elif kind == 1:
            src = pair_first.at[a, 1 - me.y] if a == 0 else pair_first.at[a, 1 - me.x]
            dst, target = plane_first.at[a], over_y if a == 0 else over_x
        else:
            src, dst = grads.at[a, me.ahead(j)], z_first.at[a, j - 1]
            target = (me.d, me.ahead(j))
        slot = kind if kind != 2 else 7 + j
        return remote(src, dst, r_send.at[a, slot], r_recv.at[a, slot], target)

    def first_z(a):
        for j in range(1, n):
            first(2, a, j).wait_recv()

        def one(i):
            y, x = lax.div(i, 2), lax.rem(i, 2)
            total = grads[a, me.f, y, x].astype(jnp.float32)
            for j in range(1, n):
                total = total + z_first[a, j - 1, y, x].astype(jnp.float32)
            z_sum[a, y, x] = total.astype(jnp.bfloat16)

        loop(4, one)
        first(0, a).start()

    def first_pair(a):
        first(0, a).wait_recv()
        for other in range(2):
            own = z_sum[a, other, me.x] if a == 0 else z_sum[a, me.y, other]
            pair_first[a, other] = add(own, pair_first[a, other])
        first(1, a).start()

    def first_plane(a):
        first(1, a).wait_recv()
        keep = me.y if a == 0 else me.x
        sums[a, me.q] = add(pair_first[a, keep], plane_first[a])
        reduce(3, 0, a).start()
        reduce(4, 0, a).start()

    def firsts(stage):
        stage(0)
        stage(1)

    def add(left, right):
        return left + right

    def stage_pair(k, a):
        m = 2 * k + a
        reduce(0, k, a).wait_recv()

        def one(i):
            f, other = lax.div(i, 2), lax.rem(i, 2)
            own = grads[m, f, other, me.x] if a == 0 else grads[m, f, me.y, other]
            pair[m, f, other] = add(own, pair[m, f, other])

        loop(2 * n, one)
        reduce(1, k, a).start()

    def stage_plane(k, a):
        m = 2 * k + a
        reduce(1, k, a).wait_recv()
        keep = me.y if a == 0 else me.x

        def one(f):
            plane[m, f] = add(pair[m, f, keep], plane[m, f])

        loop(n, one)
        for j in range(1, n):
            reduce(2, k, a, j).start()

    def stage_z(k, a):
        m = 2 * k + a
        total = plane[m, me.f].astype(jnp.float32)
        for j in range(1, n):
            reduce(2, k, a, j).wait_recv()
            total = total + z_terms[m, j - 1].astype(jnp.float32)
        sums[m, me.q] = total.astype(jnp.bfloat16)
        reduce(3, k, a).start()
        reduce(4, k, a).start()

    def stage_spread(k, a):
        reduce(3, k, a).wait_recv()
        reduce(5, k, a).start()
        reduce(4, k, a).wait_recv()
        reduce(6, k, a).start()

    def stage_last(k, a):
        reduce(5, k, a).wait_recv()
        reduce(6, k, a).wait_recv()
        reduce(7, k, a).start()
        keep(2 * k + a).start()

    def keep(m):
        return pltpu.make_async_copy(sums.at[m], sum_ref.at[me.c, m], local_sem.at[2 + m])

    def both(stage, k):
        stage(k, 0)
        stage(k, 1)

    def ahead_of(k, stage, low, high):
        @pl.when((k >= low) & (k <= high))
        def _():
            stage(k)

    def head(k):
        gathered(k)
        project(k)
        ahead_of(2 * k + 1, relay_plane, 1, last)
        ahead_of(2 * k + 2, relay_z, 2, last)
        ahead_of(k - 2, functools.partial(both, stage_pair), 1, last)
        loop(2, functools.partial(attend, k))
        ahead_of(2 * k + 2, relay_plane, 2, last)
        ahead_of(2 * k + 3, relay_z, 3, last)
        for a in range(2):
            weight_grad(k, a)

            @pl.when(k == 0)
            def _():
                for j in range(1, n):
                    first(2, a, j).start()

            @pl.when(k > 0)
            def _():
                reduce(0, k, a).start()

        ahead_of(k - 2, functools.partial(both, stage_plane), 1, last)

    loop(HEADS, head)

    def product(which, s, i):
        cols = pl.ds(pl.multiple_of(i * sub, sub), sub)
        spot = pl.ds(s * rows, rows)
        part = slice(3 * HD, 4 * HD) if which == 0 else slice(0, 3 * HD)
        total = None
        for k in range(HEADS):
            more = dot(g[k, spot, part], w[k, cols, part], CONTRACT_COLS)
            total = more if total is None else total + more
        if s == 1:
            part_out[which, :, cols] = total.astype(jnp.bfloat16)
        else:
            total = total + part_in[which, :, cols].astype(jnp.float32)
            result[which, :, cols] = total.astype(jnp.bfloat16)

    def write(which):
        dst = (out_ref, gt_ref)[which]
        return pltpu.make_async_copy(result.at[which], dst, local_sem.at[which])

    def products(which, s):
        loop(wide // sub, functools.partial(product, which, s))

    both(stage_pair, 2)
    firsts(first_z)
    products(0, 1)
    cross(3).start()
    products(1, 1)
    cross(4).start()
    both(stage_plane, 2)
    firsts(first_pair)
    both(stage_z, 1)
    both(stage_pair, 3)
    cross(3).wait_recv()
    products(0, 0)
    write(0).start()
    firsts(first_plane)
    both(stage_spread, 1)
    both(stage_z, 2)
    both(stage_plane, 3)
    cross(4).wait_recv()
    products(1, 0)
    write(1).start()
    both(stage_spread, 0)
    both(stage_last, 1)
    both(stage_spread, 2)
    both(stage_last, 0)
    both(stage_z, 3)
    both(stage_last, 2)
    both(stage_spread, 3)
    both(stage_last, 3)

    def drain(k):
        for kind in range(5):
            for j in range(1, n):
                gather(kind, k, j).wait_send()
        for a in range(2):
            for kind in (3, 4, 5, 6, 7):
                reduce(kind, k, a).wait_send()
            reduce(7, k, a).wait_recv()
            keep(2 * k + a).wait()

    def drain_plane(i):
        for a in range(2):
            reduce(0, i + 1, a).wait_send()
            reduce(1, i + 1, a).wait_send()
            for j in range(1, n):
                reduce(2, i + 1, a, j).wait_send()

    loop(HEADS, drain)
    loop(last, drain_plane)
    for a in range(2):
        first(0, a).wait_send()
        first(1, a).wait_send()
        for j in range(1, n):
            first(2, a, j).wait_send()
    for which in range(2):
        write(which).wait()
    for i in range(5):
        cross(i).wait_send()


def layer(n, tokens, cotangent, w_qkv, w_out, doc_blocks):
    rows, wide = tokens.shape
    shard = wide // n
    quarter = shard // 4
    subs = 2 * HEADS
    anywhere = pl.BlockSpec(memory_space=pl.ANY)

    def room(*shape):
        return pltpu.VMEM(shape, jnp.bfloat16)

    dma = pltpu.SemaphoreType.DMA
    return pl.pallas_call(
        functools.partial(layer_kernel, n),
        out_shape=[
            jax.ShapeDtypeStruct((2, subs, 4, quarter, 2 * HD), jnp.bfloat16),
            jax.ShapeDtypeStruct((rows, wide), jnp.bfloat16),
            jax.ShapeDtypeStruct((rows, wide), jnp.bfloat16),
        ],
        in_specs=[anywhere] * 4 + [pl.BlockSpec(memory_space=pltpu.SMEM)],
        out_specs=[anywhere] * 3,
        scratch_shapes=[
            room(2, rows, wide),
            room(2, rows, wide),
            room(wide, 2 * rows),
            room(wide, 2 * rows),
            room(2, rows, rows),
            room(HEADS, wide, 4 * HD),
            room(2, rows, 4 * HD),
            room(HEADS, 2 * rows, 4 * HD),
            room(subs, n, 2, 2, quarter, 2 * HD),
            room(subs, n, 2, quarter, 2 * HD),
            room(subs, n, quarter, 2 * HD),
            room(subs, n - 1, quarter, 2 * HD),
            room(2, rows, wide),
            room(2, rows, wide),
            room(2, rows, wide),
            room(subs, 4, quarter, 2 * HD),
            room(2, n - 1, 2, 2, quarter, 2 * HD),
            room(2, 2, 2, quarter, 2 * HD),
            room(2, 2, quarter, 2 * HD),
            room(2, quarter, 2 * HD),
            dma((HEADS, 5 * (n - 1))),
            dma((HEADS, 5 * (n - 1))),
            dma((subs, 7 + n)),
            dma((subs, 7 + n)),
            dma((5,)),
            dma((5,)),
            dma((2 + 4 * HEADS,)),
        ],
        compiler_params=pltpu.CompilerParams(
            collective_id=0, has_side_effects=True, vmem_limit_bytes=56 << 20
        ),
        name="layer",
    )(tokens, cotangent, w_qkv, w_out, doc_blocks)


def finish_kernel(norm, sum_ref, out_in, gt_in, out_ref, gt_ref, gq_ref, go_ref):
    out_ref[...] = out_in[...]
    gt_ref[...] = gt_in[...]
    width = go_ref.shape[1]
    for c in range(2):
        for m in range(2 * HEADS):
            head = c * HEADS + m // 2
            for i in range(2):
                value = sum_ref[c, m, 0, :, i * HD : (i + 1) * HD].astype(jnp.float32) * norm
                p = (m % 2) * 2 + i
                if p < 3:
                    gq_ref[:, p * width + head * HD : p * width + (head + 1) * HD] = value
                else:
                    go_ref[:, head * HD : (head + 1) * HD] = value


def finish(norm, sums, output, grad_tokens):
    rows, wide = output.shape
    quarter, width = sums.shape[3], 2 * HEADS * HD
    act = pl.BlockSpec((rows // 4, wide), lambda q: (q, 0))
    return pl.pallas_call(
        functools.partial(finish_kernel, norm),
        grid=(4,),
        out_shape=[
            jax.ShapeDtypeStruct((rows, wide), jnp.bfloat16),
            jax.ShapeDtypeStruct((rows, wide), jnp.bfloat16),
            jax.ShapeDtypeStruct((4 * quarter, 3 * width), jnp.float32),
            jax.ShapeDtypeStruct((4 * quarter, width), jnp.float32),
        ],
        in_specs=[
            pl.BlockSpec((2, 2 * HEADS, 1, quarter, 2 * HD), lambda q: (0, 0, q, 0, 0)),
            act,
            act,
        ],
        out_specs=[
            act,
            act,
            pl.BlockSpec((quarter, 3 * width), lambda q: (q, 0)),
            pl.BlockSpec((quarter, width), lambda q: (q, 0)),
        ],
        compiler_params=pltpu.CompilerParams(vmem_limit_bytes=60 << 20),
        name="finish",
    )(sums, output, grad_tokens)


def chip_body(tokens, w_qkv, w_out, doc_blocks, cotangent):
    n = lax.axis_size("fsdp")
    all_devices = lax.axis_size("dp") * n
    sums, output, grad_tokens = layer(n, tokens, cotangent, w_qkv, w_out, doc_blocks)
    norm_factor = 1.0 / math.sqrt(tokens.shape[0] * all_devices)
    return tuple(finish(norm_factor, sums, output, grad_tokens))


def solution(mesh):
    placed = (
        P(("dp", "fsdp"), None),
        P("fsdp", None),
        P("fsdp", None),
        P(("dp", "fsdp"), None),
        P(("dp", "fsdp"), None),
    )
    in_plane = mesh.shape["dp"] == 8 and mesh.shape["fsdp"] == 4
    return jax.shard_map(
        chip_body if in_plane else body,
        mesh=mesh,
        in_specs=placed,
        out_specs=(
            P(("dp", "fsdp"), None),
            P(("dp", "fsdp"), None),
            P("fsdp", None),
            P("fsdp", None),
        ),
        check_vma=False,
    )
```

```python
import functools
import math

import jax
import jax.numpy as jnp
from jax import lax
from jax.experimental import pallas as pl
from jax.experimental.pallas import tpu as pltpu
from jax.sharding import PartitionSpec as P

H = 8


NEG_FILL = -1e30
CONTRACT_ROWS = (((0,), (0,)), ((), ()))
CONTRACT_COLS = (((1,), (1,)), ((), ()))


def row_mask(doc_ids, row_count):
    block_len = row_count // doc_ids.shape[0]
    doc_rows = jnp.repeat(doc_ids, block_len, total_repeat_length=row_count)
    position = jnp.arange(row_count, dtype=jnp.int32)
    causal = position[None, :] <= position[:, None]
    return causal & (doc_rows[None, :] == doc_rows[:, None])


def split_heads(matrix, head_count):
    return matrix.reshape(matrix.shape[0], head_count, matrix.shape[1] // head_count)


def attend_forward(query_rows, key_rows, value_rows, allowed, head_count):
    row_count = query_rows.shape[0]
    query_heads = split_heads(query_rows, head_count)
    key_heads = split_heads(key_rows, head_count)
    value_heads = split_heads(value_rows, head_count)
    score_scale = query_heads.shape[2] ** (-0.5)
    scores = (
        jnp.einsum("qhd,khd->hqk", query_heads, key_heads, preferred_element_type=jnp.float32)
        * score_scale
    )
    scores = jnp.where(allowed[None], scores, NEG_FILL)
    highest = jnp.max(scores, axis=-1, keepdims=True)
    expvals = jnp.exp(scores - highest)
    attn_probs = expvals / jnp.sum(expvals, axis=-1, keepdims=True)
    probs_half = attn_probs.astype(jnp.bfloat16)
    mixed = jnp.einsum("hqk,khd->qhd", probs_half, value_heads, preferred_element_type=jnp.float32)
    return (mixed.astype(jnp.bfloat16).reshape(row_count, -1), attn_probs, probs_half)


def attend_backward(
    query_rows, key_rows, value_rows, attn_probs, probs_half, grad_mixed, head_count
):
    row_count = query_rows.shape[0]
    query_heads = split_heads(query_rows, head_count)
    key_heads = split_heads(key_rows, head_count)
    value_heads = split_heads(value_rows, head_count)
    grad_heads = split_heads(grad_mixed, head_count)
    score_scale = query_heads.shape[2] ** (-0.5)
    grad_probs = jnp.einsum(
        "qhd,khd->hqk", grad_heads, value_heads, preferred_element_type=jnp.float32
    )
    grad_values = jnp.einsum(
        "hqk,qhd->khd", probs_half, grad_heads, preferred_element_type=jnp.float32
    )
    inner = jnp.sum(attn_probs * grad_probs, axis=-1, keepdims=True)
    grad_scores = (attn_probs * (grad_probs - inner)).astype(jnp.bfloat16)
    grad_queries = (
        jnp.einsum("hqk,khd->qhd", grad_scores, key_heads, preferred_element_type=jnp.float32)
        * score_scale
    )
    grad_keys = (
        jnp.einsum("hqk,qhd->khd", grad_scores, query_heads, preferred_element_type=jnp.float32)
        * score_scale
    )
    pieces_list = [grad_queries, grad_keys, grad_values]
    return jnp.concatenate(
        [p.astype(jnp.bfloat16).reshape(row_count, -1) for p in pieces_list], axis=1
    )


def body(tokens, w_qkv, w_out, doc_blocks, cotangent):
    row_count = tokens.shape[0]
    head_width = w_out.shape[1]
    head_count = H
    all_devices = lax.axis_size("dp") * lax.axis_size("fsdp")
    allowed = row_mask(doc_blocks[0], row_count)
    columns = tokens
    qkv = jnp.dot(
        columns,
        lax.all_gather(w_qkv, "fsdp", axis=0, tiled=True),
        preferred_element_type=jnp.float32,
    ).astype(jnp.bfloat16)
    query_rows = qkv[:, :head_width]
    key_rows = qkv[:, head_width : 2 * head_width]
    value_rows = qkv[:, 2 * head_width :]
    mixed, attn_probs, probs_half = attend_forward(
        query_rows, key_rows, value_rows, allowed, head_count
    )
    output = lax.dot_general(
        mixed,
        lax.all_gather(w_out, "fsdp", axis=0, tiled=True),
        CONTRACT_COLS,
        preferred_element_type=jnp.float32,
    )
    columns = cotangent
    grad_mixed = jnp.dot(
        columns,
        lax.all_gather(w_out, "fsdp", axis=0, tiled=True),
        preferred_element_type=jnp.float32,
    ).astype(jnp.bfloat16)
    output = output.astype(jnp.bfloat16)
    grad_qkv = attend_backward(
        query_rows, key_rows, value_rows, attn_probs, probs_half, grad_mixed, head_count
    )
    grad_tokens = lax.dot_general(
        grad_qkv,
        lax.all_gather(w_qkv, "fsdp", axis=0, tiled=True),
        CONTRACT_COLS,
        preferred_element_type=jnp.float32,
    )
    grad_tokens = grad_tokens.astype(jnp.bfloat16)
    first_term = lax.dot_general(
        tokens, grad_qkv, CONTRACT_ROWS, preferred_element_type=jnp.float32
    )
    second_term = lax.dot_general(
        cotangent, mixed, CONTRACT_ROWS, preferred_element_type=jnp.float32
    )
    partial_grad = lax.psum_scatter(
        jnp.concatenate([first_term, second_term], axis=1), "fsdp", scatter_dimension=0, tiled=True
    )
    summed = lax.psum(partial_grad, "dp")
    norm_factor = 1.0 / math.sqrt(row_count * all_devices)
    grad_w_qkv = summed[:, : 3 * head_width] * norm_factor
    grad_w_out = summed[:, 3 * head_width :] * norm_factor
    return (output, grad_tokens, grad_w_qkv, grad_w_out)


MESH = pl.DeviceIdType.MESH
HEADS = 4
HD = 128
PLAIN = (((1,), (0,)), ((), ()))


class Place:
    def __init__(self, fsdp_size):
        self.d, self.f = lax.axis_index("dp"), lax.axis_index("fsdp")
        self.c = lax.rem(self.d, 2)
        chip = lax.div(self.d, 2)
        self.x, self.y = lax.rem(chip, 2), lax.div(chip, 2)
        self.dx = self.dp_of(self.y, 1 - self.x, self.c)
        self.dy = self.dp_of(1 - self.y, self.x, self.c)
        self.dc = self.dp_of(self.y, self.x, 1 - self.c)
        self.q = self.y * 2 + self.x
        self.qx = self.y * 2 + 1 - self.x
        self.qy = (1 - self.y) * 2 + self.x
        self.n = fsdp_size

    def dp_of(self, y, x, c):
        return (y * 2 + x) * 2 + c

    def ahead(self, j):
        return lax.rem(self.f + j, self.n)

    def behind(self, j):
        return lax.rem(self.f + self.n - j, self.n)

    def barrier(self):
        sem = pltpu.get_barrier_semaphore()
        targets = [(self.dx, self.f), (self.dy, self.f), (self.dc, self.f)]
        targets += [(self.d, self.ahead(j)) for j in range(1, self.n)]
        for target in targets:
            pl.semaphore_signal(sem, inc=1, device_id=target, device_id_type=MESH)
        pl.semaphore_wait(sem, len(targets))


def dot(left, right, dims=PLAIN):
    return lax.dot_general(left, right, dims, preferred_element_type=jnp.float32)


def remote(src, dst, send_sem, recv_sem, target):
    return pltpu.make_async_remote_copy(
        src_ref=src,
        dst_ref=dst,
        send_sem=send_sem,
        recv_sem=recv_sem,
        device_id=target,
        device_id_type=MESH,
    )


def loop(count, work):
    def step(i, carry):
        work(i)
        return carry

    lax.fori_loop(0, count, step, 0)


def layer_kernel(
    n,
    tok_ref,
    cot_ref,
    wq_ref,
    wo_ref,
    doc_ref,
    sum_ref,
    out_ref,
    gt_ref,
    toks,
    cots,
    toks_t,
    cots_t,
    bias,
    w,
    x,
    g,
    grads,
    pair,
    plane,
    z_terms,
    part_out,
    part_in,
    result,
    sums,
    z_first,
    z_sum,
    pair_first,
    plane_first,
    g_send,
    g_recv,
    r_send,
    r_recv,
    c_send,
    c_recv,
    local_sem,
):
    me = Place(n)
    rows = toks.shape[1]
    wide = toks.shape[2]
    shard = wide // n
    quarter = shard // 4
    half = quarter // 2
    sub = 2 * HD
    last = HEADS - 1
    scale = HD ** (-0.5)

    def load_act(i):
        src, dst = ((tok_ref, toks), (cot_ref, cots))[i]
        return pltpu.make_async_copy(src, dst.at[0], local_sem.at[i])

    def load_w(k, p):
        src, base = (wq_ref, p * wo_ref.shape[1]) if p < 3 else (wo_ref, 0)
        first = pl.multiple_of(base + (me.c * HEADS + k) * HD, HD)
        spot = pl.ds(pl.multiple_of(me.f * shard, shard), shard)
        return pltpu.make_async_copy(
            src.at[:, pl.ds(first, HD)],
            w.at[k, spot, pl.ds(p * HD, HD)],
            local_sem.at[2 + k * 4 + p],
        )

    for k in range(HEADS):
        for p in range(4):
            load_w(k, p).start()
        if k < 2:
            load_act(k).start()
    me.barrier()

    def span(k, f, q, first, count):
        start = pl.multiple_of(f * shard + q * quarter + first, half)
        return w.at[k, pl.ds(start, count)]

    def gather(kind, k, j):
        f = me.f if kind == 0 else me.behind(j)
        q, first, count, target = (
            (me.q, 0, quarter, (me.d, me.ahead(j))),
            (me.q, 0, quarter, (me.dx, me.f)),
            (me.q, 0, quarter, (me.dy, me.f)),
            (me.qx, 0, half, (me.dy, me.f)),
            (me.qy, half, half, (me.dx, me.f)),
        )[kind]
        spot = span(k, f, q, first, count)
        slot = kind * (n - 1) + j - 1
        return remote(spot, spot, g_send.at[k, slot], g_recv.at[k, slot], target)

    for k in range(HEADS):
        for p in range(4):
            load_w(k, p).wait()
        if k < 2:
            for j in range(1, n):
                gather(0, k, j).start()

    def from_z(k, j):
        gather(0, k, j).wait_recv()
        gather(1, k, j).start()
        gather(2, k, j).start()
        if k + 2 < HEADS:
            gather(0, k + 2, j).start()

    def from_plane(k, j):
        gather(1, k, j).wait_recv()
        gather(3, k, j).start()
        gather(2, k, j).wait_recv()
        gather(4, k, j).start()

    def relay_z(k):
        for j in range(1, n):
            from_z(k, j)

    def relay_plane(k):
        for j in range(1, n):
            from_plane(k, j)

    def gathered(k):
        for j in range(1, n):
            gather(3, k, j).wait_recv()
            gather(4, k, j).wait_recv()

    def cross(i):
        src, dst = (
            (toks.at[0], toks.at[1]),
            (cots.at[0], cots.at[1]),
            (bias.at[0], bias.at[1]),
            (part_out.at[0], part_in.at[0]),
            (part_out.at[1], part_in.at[1]),
        )[i]
        return remote(src, dst, c_send.at[i], c_recv.at[i], (me.dc, me.f))

    for i in range(2):
        load_act(i).wait()
        cross(i).start()

    block = rows // doc_ref.shape[1]
    key_row = lax.broadcasted_iota(jnp.int32, (rows, rows), 0)
    query_row = lax.broadcasted_iota(jnp.int32, (rows, rows), 1)

    def doc_of(row):
        ids = jnp.full(row.shape, doc_ref[0, 0], jnp.int32)
        for b in range(1, doc_ref.shape[1]):
            ids = jnp.where(row >= b * block, doc_ref[0, b], ids)
        return ids

    docs_k = doc_of(lax.broadcasted_iota(jnp.int32, (rows, HD), 0))
    docs_q = doc_of(lax.broadcasted_iota(jnp.int32, (8, rows), 1))
    same = docs_k[:, :1] == docs_q[:1, :]
    allowed = same & (key_row <= query_row)
    bias[0] = jnp.where(allowed, 0.0, NEG_FILL).astype(jnp.bfloat16)
    cross(2).start()

    def turn(s):
        def one(i):
            part = pl.ds(pl.multiple_of(i * HD, HD), HD)
            spot = pl.ds(s * rows, rows)
            toks_t[part, spot] = toks[s, :, part].T
            cots_t[part, spot] = cots[s, :, part].T

        loop(wide // HD, one)

    turn(0)
    for j in range(1, n + 1):
        if j < n:
            from_z(0, j)
        if j > 1:
            from_plane(0, j - 1)
    relay_z(1)

    def project(k, s):
        x[s, :, : 3 * HD] = dot(toks[s], w[k, :, : 3 * HD]).astype(jnp.bfloat16)
        x[s, :, 3 * HD :] = dot(cots[s], w[k, :, 3 * HD :]).astype(jnp.bfloat16)

    def attend(k, s):
        key, value = x[s, :, HD : 2 * HD], x[s, :, 2 * HD : 3 * HD]
        key_t, value_t = key.T, value.T
        grad_k, grad_v = None, None
        base = pl.multiple_of(s * rows, rows)
        for part in (1, 0):
            span_q = slice(part * rows // 2, (part + 1) * rows // 2)
            deep = (part + 1) * rows // 2
            query, gm = x[s, span_q, :HD], x[s, span_q, 3 * HD :]
            scores = dot(key[:deep], query, CONTRACT_COLS) * scale
            scores = scores + bias[s, :deep, span_q].astype(jnp.float32)
            expvals = jnp.exp(scores - jnp.max(scores, axis=0, keepdims=True))
            probs = expvals * (1.0 / jnp.sum(expvals, axis=0, keepdims=True))
            probs_half = probs.astype(jnp.bfloat16)
            mixed = dot(value_t[:, :deep], probs_half).astype(jnp.bfloat16)
            grad_probs = dot(value[:deep], gm, CONTRACT_COLS)
            inner = jnp.sum(probs * grad_probs, axis=0, keepdims=True)
            grad_scores = (probs * (grad_probs - inner)).astype(jnp.bfloat16)
            grad_q = (dot(key_t[:, :deep], grad_scores) * scale).astype(jnp.bfloat16)
            spot = pl.ds(base + part * (rows // 2), rows // 2)
            g[k, spot, :HD] = grad_q.T
            g[k, spot, 3 * HD :] = mixed.T
            more_k, more_v = dot(grad_scores, query), dot(probs_half, gm)
            if part == 1:
                grad_k, grad_v = more_k, more_v
            else:
                low = pl.ds(base, rows // 2)
                high = pl.ds(base + rows // 2, rows // 2)
                more_k, more_v = more_k + grad_k[:deep], more_v + grad_v[:deep]
                g[k, low, HD : 2 * HD] = (more_k * scale).astype(jnp.bfloat16)
                g[k, low, 2 * HD : 3 * HD] = more_v.astype(jnp.bfloat16)
                g[k, high, HD : 2 * HD] = (grad_k[deep:] * scale).astype(jnp.bfloat16)
                g[k, high, 2 * HD : 3 * HD] = grad_v[deep:].astype(jnp.bfloat16)

    def weight_grad(k, a):
        m = 2 * k + a

        def one(i):
            deep = 2 * shard
            spot = pl.ds(pl.multiple_of(i * deep, deep), deep)
            fs = pl.ds(2 * i, 2)
            if a == 0:
                total = dot(toks_t[spot, :], g[k, :, :sub]).astype(jnp.bfloat16)
                grads[m, fs] = total.reshape(2, 2, 2, quarter, sub)
            else:
                left = dot(toks_t[spot, :], g[k, :, sub : 3 * HD]).astype(jnp.bfloat16)
                right = dot(cots_t[spot, :], g[k, :, 3 * HD :]).astype(jnp.bfloat16)
                grads[m, fs, :, :, :, :HD] = left.reshape(2, 2, 2, quarter, HD)
                grads[m, fs, :, :, :, HD:] = right.reshape(2, 2, 2, quarter, HD)

        loop(n // 2, one)

    def columns_of(cut):
        return slice(None) if cut is None else pl.ds(cut * HD, HD)

    def reduce(kind, k, a, j=0, cut=None):
        m, cols = 2 * k + a, columns_of(cut)
        over_x, over_y = (me.dx, me.f), (me.dy, me.f)
        everything = pl.ds(0, quarter)
        if kind == 0:
            src = (
                grads.at[m, :, :, 1 - me.x, :, cols]
                if a == 0
                else grads.at[m, :, 1 - me.y, :, :, cols]
            )
            dst, target = pair.at[m, :, :, :, cols], over_x if a == 0 else over_y
        elif kind == 1:
            other = 1 - me.y if a == 0 else 1 - me.x
            src, dst = pair.at[m, :, other, :, cols], plane.at[m, :, :, cols]
            target = over_y if a == 0 else over_x
        elif kind == 2:
            src, dst = plane.at[m, me.ahead(j), :, cols], z_terms.at[m, j - 1, :, cols]
            target = (me.d, me.ahead(j))
        elif kind == 7:
            src, dst = sums.at[m, :, :, cols], sum_ref.at[me.c, m, :, :, cols]
            target = (me.dc, me.f)
        else:
            q, span_r, target = (
                (me.q, everything, over_x),
                (me.q, everything, over_y),
                (me.qx, pl.ds(0, half), over_y),
                (me.qy, pl.ds(half, half), over_x),
            )[kind - 3]
            src = sums.at[m, q, span_r, cols]
            dst = src
        slot = (kind if kind != 2 else 7 + j) + (0 if cut in (None, 0) else 7 + n)
        return remote(src, dst, r_send.at[m, slot], r_recv.at[m, slot], target)

    def first(kind, a, j=0):
        over_x, over_y = (me.dx, me.f), (me.dy, me.f)
        if kind == 0:
            src = z_sum.at[a, :, 1 - me.x] if a == 0 else z_sum.at[a, 1 - me.y]
            dst, target = pair_first.at[a], over_x if a == 0 else over_y
        elif kind == 1:
            src = pair_first.at[a, 1 - me.y] if a == 0 else pair_first.at[a, 1 - me.x]
            dst, target = plane_first.at[a], over_y if a == 0 else over_x
        else:
            src, dst = grads.at[a, me.ahead(j)], z_first.at[a, j - 1]
            target = (me.d, me.ahead(j))
        slot = kind if kind != 2 else 7 + j
        return remote(src, dst, r_send.at[a, slot], r_recv.at[a, slot], target)

    def first_z(a):
        for j in range(1, n):
            first(2, a, j).wait_recv()

        def one(i):
            y, x = lax.div(i, 2), lax.rem(i, 2)
            total = grads[a, me.f, y, x].astype(jnp.float32)
            for j in range(1, n):
                total = total + z_first[a, j - 1, y, x].astype(jnp.float32)
            z_sum[a, y, x] = total.astype(jnp.bfloat16)

        loop(4, one)
        first(0, a).start()

    def first_pair(a):
        first(0, a).wait_recv()
        for other in range(2):
            own = z_sum[a, other, me.x] if a == 0 else z_sum[a, me.y, other]
            pair_first[a, other] = add(own, pair_first[a, other])
        first(1, a).start()

    def first_plane(a):
        first(1, a).wait_recv()
        keep = me.y if a == 0 else me.x
        sums[a, me.q] = add(pair_first[a, keep], plane_first[a])
        reduce(3, 0, a).start()
        reduce(4, 0, a).start()

    def firsts(stage):
        stage(0)
        stage(1)

    def add(left, right):
        return left + right

    def stage_pair(k, a, cut=None):
        m, cols = 2 * k + a, columns_of(cut)
        reduce(0, k, a, 0, cut).wait_recv()

        def one(i):
            f, other = lax.div(i, 2), lax.rem(i, 2)
            y, x = (other, me.x) if a == 0 else (me.y, other)
            total = add(grads[m, f, y, x, :, cols], pair[m, f, other, :, cols])
            pair[m, f, other, :, cols] = total

        loop(2 * n, one)
        reduce(1, k, a, 0, cut).start()

    def stage_plane(k, a, cut=None):
        m, cols = 2 * k + a, columns_of(cut)
        reduce(1, k, a, 0, cut).wait_recv()
        stay = me.y if a == 0 else me.x

        def one(f):
            plane[m, f, :, cols] = add(pair[m, f, stay, :, cols], plane[m, f, :, cols])

        loop(n, one)
        for j in range(1, n):
            reduce(2, k, a, j, cut).start()

    def stage_z(k, a, cut=None):
        m, cols = 2 * k + a, columns_of(cut)
        total = plane[m, me.f, :, cols].astype(jnp.float32)
        for j in range(1, n):
            reduce(2, k, a, j, cut).wait_recv()
            total = total + z_terms[m, j - 1, :, cols].astype(jnp.float32)
        sums[m, me.q, :, cols] = total.astype(jnp.bfloat16)
        reduce(3, k, a, 0, cut).start()
        reduce(4, k, a, 0, cut).start()

    def stage_spread(k, a, cut=None):
        reduce(3, k, a, 0, cut).wait_recv()
        reduce(5, k, a, 0, cut).start()
        reduce(4, k, a, 0, cut).wait_recv()
        reduce(6, k, a, 0, cut).start()

    def stage_last(k, a, cut=None):
        reduce(5, k, a, 0, cut).wait_recv()
        reduce(6, k, a, 0, cut).wait_recv()
        reduce(7, k, a, 0, cut).start()
        if cut != 0:
            keep(2 * k + a).start()

    def keep(m):
        return pltpu.make_async_copy(sums.at[m], sum_ref.at[me.c, m], local_sem.at[2 + m])

    def both(stage, k, cut=None):
        stage(k, 0, cut)
        stage(k, 1, cut)

    def when(condition, *work):
        @pl.when(condition)
        def _():
            for one in work:
                one()

    def partner():
        for i in range(3):
            cross(i).wait_recv()
        turn(1)

    call = functools.partial

    def head(k):
        gathered(k)

        def sequence(s):
            when((k == 0) & (s == 1), partner)
            project(k, s)
            when((k > 2) & (s == 0), call(both, stage_pair, k - 2))
            attend(k, s)
            when((k == 0) & (s == 0), call(relay_plane, 1))
            when((k == 0) & (s == 0), call(relay_z, 2))
            when((k == 1) & (s == 1), call(relay_plane, 3))

        loop(2, sequence)

        def columns(a):
            weight_grad(k, a)

            @pl.when(k == 0)
            def _():
                for j in range(1, n):
                    first(2, a, j).start()

            @pl.when((k > 0) & (k < last))
            def _():
                reduce(0, k, a).start()

        columns(0)
        columns(1)
        when(k == 0, call(relay_z, 3))
        when(k == 0, call(relay_plane, 2))
        when(k > 2, call(both, stage_plane, k - 2))

    loop(HEADS, head)
    for cut in range(2):
        for a in range(2):
            reduce(0, last, a, 0, cut).start()

    def product(which, s, i):
        cols = pl.ds(pl.multiple_of(i * sub, sub), sub)
        spot = pl.ds(s * rows, rows)
        part = slice(3 * HD, 4 * HD) if which == 0 else slice(0, 3 * HD)
        total = None
        for k in range(HEADS):
            more = dot(g[k, spot, part], w[k, cols, part], CONTRACT_COLS)
            total = more if total is None else total + more
        if s == 1:
            part_out[which, :, cols] = total.astype(jnp.bfloat16)
        else:
            total = total + part_in[which, :, cols].astype(jnp.float32)
            result[which, :, cols] = total.astype(jnp.bfloat16)

    def write(which):
        dst = (out_ref, gt_ref)[which]
        return pltpu.make_async_copy(result.at[which], dst, local_sem.at[which])

    def products(which, s):
        loop(wide // sub, functools.partial(product, which, s))

    both(stage_pair, 2)
    products(0, 1)
    cross(3).start()
    firsts(first_z)
    both(stage_z, 1)
    both(stage_plane, 2)
    both(stage_pair, last, 0)
    both(stage_pair, last, 1)
    products(1, 1)
    cross(4).start()
    firsts(first_pair)
    both(stage_plane, last, 0)
    both(stage_plane, last, 1)
    both(stage_spread, 1)
    both(stage_z, 2)
    firsts(first_plane)
    both(stage_z, last, 0)
    both(stage_spread, 2)
    both(stage_z, last, 1)
    both(stage_spread, 0)
    cross(3).wait_recv()
    products(0, 0)
    write(0).start()
    both(stage_spread, last, 0)
    both(stage_last, 1)
    both(stage_spread, last, 1)
    cross(4).wait_recv()
    products(1, 0)
    write(1).start()
    both(stage_last, 2)
    both(stage_last, 0)
    both(stage_last, last, 0)
    both(stage_last, last, 1)

    def drain_gather(k):
        for kind in range(5):
            for j in range(1, n):
                gather(kind, k, j).wait_send()

    def drain(k, cut=None, kinds=(0, 1, 3, 4, 5, 6, 7)):
        for a in range(2):
            for kind in kinds:
                reduce(kind, k, a, 0, cut).wait_send()
            if 0 in kinds:
                for j in range(1, n):
                    reduce(2, k, a, j, cut).wait_send()
            reduce(7, k, a, 0, cut).wait_recv()
            if cut != 0:
                keep(2 * k + a).wait()

    loop(HEADS, drain_gather)
    drain(0, None, (3, 4, 5, 6, 7))
    loop(last - 1, lambda i: drain(i + 1))
    drain(last, 0)
    drain(last, 1)
    for a in range(2):
        first(0, a).wait_send()
        first(1, a).wait_send()
        for j in range(1, n):
            first(2, a, j).wait_send()
    for which in range(2):
        write(which).wait()
    for i in range(5):
        cross(i).wait_send()


def layer(n, tokens, cotangent, w_qkv, w_out, doc_blocks):
    rows, wide = tokens.shape
    shard = wide // n
    quarter = shard // 4
    subs = 2 * HEADS
    anywhere = pl.BlockSpec(memory_space=pl.ANY)

    def room(*shape):
        return pltpu.VMEM(shape, jnp.bfloat16)

    dma = pltpu.SemaphoreType.DMA
    return pl.pallas_call(
        functools.partial(layer_kernel, n),
        out_shape=[
            jax.ShapeDtypeStruct((2, subs, 4, quarter, 2 * HD), jnp.bfloat16),
            jax.ShapeDtypeStruct((rows, wide), jnp.bfloat16),
            jax.ShapeDtypeStruct((rows, wide), jnp.bfloat16),
        ],
        in_specs=[anywhere] * 4 + [pl.BlockSpec(memory_space=pltpu.SMEM)],
        out_specs=[anywhere] * 3,
        scratch_shapes=[
            room(2, rows, wide),
            room(2, rows, wide),
            room(wide, 2 * rows),
            room(wide, 2 * rows),
            room(2, rows, rows),
            room(HEADS, wide, 4 * HD),
            room(2, rows, 4 * HD),
            room(HEADS, 2 * rows, 4 * HD),
            room(subs, n, 2, 2, quarter, 2 * HD),
            room(subs, n, 2, quarter, 2 * HD),
            room(subs, n, quarter, 2 * HD),
            room(subs, n - 1, quarter, 2 * HD),
            room(2, rows, wide),
            room(2, rows, wide),
            room(2, rows, wide),
            room(subs, 4, quarter, 2 * HD),
            room(2, n - 1, 2, 2, quarter, 2 * HD),
            room(2, 2, 2, quarter, 2 * HD),
            room(2, 2, quarter, 2 * HD),
            room(2, quarter, 2 * HD),
            dma((HEADS, 5 * (n - 1))),
            dma((HEADS, 5 * (n - 1))),
            dma((subs, 2 * (7 + n))),
            dma((subs, 2 * (7 + n))),
            dma((5,)),
            dma((5,)),
            dma((2 + 4 * HEADS,)),
        ],
        compiler_params=pltpu.CompilerParams(
            collective_id=0, has_side_effects=True, vmem_limit_bytes=56 << 20
        ),
        name="layer",
    )(tokens, cotangent, w_qkv, w_out, doc_blocks)


def finish_kernel(
    norm, sum_ref, out_in, gt_in, out_ref, gt_ref, gq_ref, go_ref, sums, acts, gq, go, load_sem, store_sem
):
    width, quarter = go.shape[1], sums.shape[3]

    def load(q):
        return pltpu.make_async_copy(sum_ref.at[:, :, q], sums.at[:, :, q], load_sem.at[q])

    def store(q, i):
        src, dst = ((gq, gq_ref), (go, go_ref))[i]
        span = pl.ds(q * quarter, quarter)
        return pltpu.make_async_copy(src.at[span], dst.at[span], store_sem.at[q, i])

    def act(i, leave):
        src, dst = ((out_in, out_ref), (gt_in, gt_ref))[i]
        if leave:
            return pltpu.make_async_copy(acts.at[i], dst, store_sem.at[4, i])
        return pltpu.make_async_copy(src, acts.at[i], load_sem.at[4 + i])

    for i in range(2):
        act(i, False).start()
    for q in range(4):
        load(q).start()
    for i in range(2):
        act(i, False).wait()
        act(i, True).start()

    for q in range(4):
        load(q).wait()
        span = pl.ds(q * quarter, quarter)
        for c in range(2):
            for m in range(2 * HEADS):
                head = c * HEADS + m // 2
                for i in range(2):
                    value = sums[c, m, q, :, i * HD : (i + 1) * HD].astype(jnp.float32) * norm
                    p = (m % 2) * 2 + i
                    if p < 3:
                        gq[span, p * width + head * HD : p * width + (head + 1) * HD] = value
                    else:
                        go[span, head * HD : (head + 1) * HD] = value
        for i in range(2):
            store(q, i).start()
    for q in range(4):
        for i in range(2):
            store(q, i).wait()
    for i in range(2):
        act(i, True).wait()


def finish(norm, sums, output, grad_tokens):
    rows, wide = output.shape
    quarter, width = sums.shape[3], 2 * HEADS * HD
    anywhere = pl.BlockSpec(memory_space=pl.ANY)
    grads = [(4 * quarter, 3 * width), (4 * quarter, width)]
    return pl.pallas_call(
        functools.partial(finish_kernel, norm),
        out_shape=[jax.ShapeDtypeStruct((rows, wide), jnp.bfloat16)] * 2
        + [jax.ShapeDtypeStruct(shape, jnp.float32) for shape in grads],
        in_specs=[anywhere] * 3,
        out_specs=[anywhere] * 4,
        scratch_shapes=[pltpu.VMEM(shape, jnp.bfloat16) for shape in (sums.shape, (2, rows, wide))]
        + [pltpu.VMEM(shape, jnp.float32) for shape in grads]
        + [pltpu.SemaphoreType.DMA((6,)), pltpu.SemaphoreType.DMA((5, 2))],
        compiler_params=pltpu.CompilerParams(vmem_limit_bytes=60 << 20),
        name="finish",
    )(sums, output, grad_tokens)


def chip_body(tokens, w_qkv, w_out, doc_blocks, cotangent):
    n = lax.axis_size("fsdp")
    all_devices = lax.axis_size("dp") * n
    sums, output, grad_tokens = layer(n, tokens, cotangent, w_qkv, w_out, doc_blocks)
    norm_factor = 1.0 / math.sqrt(tokens.shape[0] * all_devices)
    return tuple(finish(norm_factor, sums, output, grad_tokens))


def solution(mesh):
    placed = (
        P(("dp", "fsdp"), None),
        P("fsdp", None),
        P("fsdp", None),
        P(("dp", "fsdp"), None),
        P(("dp", "fsdp"), None),
    )
    in_plane = mesh.shape["dp"] == 8 and mesh.shape["fsdp"] == 4
    return jax.shard_map(
        chip_body if in_plane else body,
        mesh=mesh,
        in_specs=placed,
        out_specs=(
            P(("dp", "fsdp"), None),
            P(("dp", "fsdp"), None),
            P("fsdp", None),
            P("fsdp", None),
        ),
        check_vma=False,
    )
```

```python
import functools
import math

import jax
import jax.numpy as jnp
from jax import lax
from jax.experimental import pallas as pl
from jax.experimental.pallas import tpu as pltpu
from jax.sharding import PartitionSpec as P

H = 8


NEG_FILL = -1e30
CONTRACT_ROWS = (((0,), (0,)), ((), ()))
CONTRACT_COLS = (((1,), (1,)), ((), ()))


def row_mask(doc_ids, row_count):
    block_len = row_count // doc_ids.shape[0]
    doc_rows = jnp.repeat(doc_ids, block_len, total_repeat_length=row_count)
    position = jnp.arange(row_count, dtype=jnp.int32)
    causal = position[None, :] <= position[:, None]
    return causal & (doc_rows[None, :] == doc_rows[:, None])


def split_heads(matrix, head_count):
    return matrix.reshape(matrix.shape[0], head_count, matrix.shape[1] // head_count)


def attend_forward(query_rows, key_rows, value_rows, allowed, head_count):
    row_count = query_rows.shape[0]
    query_heads = split_heads(query_rows, head_count)
    key_heads = split_heads(key_rows, head_count)
    value_heads = split_heads(value_rows, head_count)
    score_scale = query_heads.shape[2] ** (-0.5)
    scores = (
        jnp.einsum("qhd,khd->hqk", query_heads, key_heads, preferred_element_type=jnp.float32)
        * score_scale
    )
    scores = jnp.where(allowed[None], scores, NEG_FILL)
    highest = jnp.max(scores, axis=-1, keepdims=True)
    expvals = jnp.exp(scores - highest)
    attn_probs = expvals / jnp.sum(expvals, axis=-1, keepdims=True)
    probs_half = attn_probs.astype(jnp.bfloat16)
    mixed = jnp.einsum("hqk,khd->qhd", probs_half, value_heads, preferred_element_type=jnp.float32)
    return (mixed.astype(jnp.bfloat16).reshape(row_count, -1), attn_probs, probs_half)


def attend_backward(
    query_rows, key_rows, value_rows, attn_probs, probs_half, grad_mixed, head_count
):
    row_count = query_rows.shape[0]
    query_heads = split_heads(query_rows, head_count)
    key_heads = split_heads(key_rows, head_count)
    value_heads = split_heads(value_rows, head_count)
    grad_heads = split_heads(grad_mixed, head_count)
    score_scale = query_heads.shape[2] ** (-0.5)
    grad_probs = jnp.einsum(
        "qhd,khd->hqk", grad_heads, value_heads, preferred_element_type=jnp.float32
    )
    grad_values = jnp.einsum(
        "hqk,qhd->khd", probs_half, grad_heads, preferred_element_type=jnp.float32
    )
    inner = jnp.sum(attn_probs * grad_probs, axis=-1, keepdims=True)
    grad_scores = (attn_probs * (grad_probs - inner)).astype(jnp.bfloat16)
    grad_queries = (
        jnp.einsum("hqk,khd->qhd", grad_scores, key_heads, preferred_element_type=jnp.float32)
        * score_scale
    )
    grad_keys = (
        jnp.einsum("hqk,qhd->khd", grad_scores, query_heads, preferred_element_type=jnp.float32)
        * score_scale
    )
    pieces_list = [grad_queries, grad_keys, grad_values]
    return jnp.concatenate(
        [p.astype(jnp.bfloat16).reshape(row_count, -1) for p in pieces_list], axis=1
    )


def body(tokens, w_qkv, w_out, doc_blocks, cotangent):
    row_count = tokens.shape[0]
    head_width = w_out.shape[1]
    head_count = H
    all_devices = lax.axis_size("dp") * lax.axis_size("fsdp")
    allowed = row_mask(doc_blocks[0], row_count)
    columns = tokens
    qkv = jnp.dot(
        columns,
        lax.all_gather(w_qkv, "fsdp", axis=0, tiled=True),
        preferred_element_type=jnp.float32,
    ).astype(jnp.bfloat16)
    query_rows = qkv[:, :head_width]
    key_rows = qkv[:, head_width : 2 * head_width]
    value_rows = qkv[:, 2 * head_width :]
    mixed, attn_probs, probs_half = attend_forward(
        query_rows, key_rows, value_rows, allowed, head_count
    )
    output = lax.dot_general(
        mixed,
        lax.all_gather(w_out, "fsdp", axis=0, tiled=True),
        CONTRACT_COLS,
        preferred_element_type=jnp.float32,
    )
    columns = cotangent
    grad_mixed = jnp.dot(
        columns,
        lax.all_gather(w_out, "fsdp", axis=0, tiled=True),
        preferred_element_type=jnp.float32,
    ).astype(jnp.bfloat16)
    output = output.astype(jnp.bfloat16)
    grad_qkv = attend_backward(
        query_rows, key_rows, value_rows, attn_probs, probs_half, grad_mixed, head_count
    )
    grad_tokens = lax.dot_general(
        grad_qkv,
        lax.all_gather(w_qkv, "fsdp", axis=0, tiled=True),
        CONTRACT_COLS,
        preferred_element_type=jnp.float32,
    )
    grad_tokens = grad_tokens.astype(jnp.bfloat16)
    first_term = lax.dot_general(
        tokens, grad_qkv, CONTRACT_ROWS, preferred_element_type=jnp.float32
    )
    second_term = lax.dot_general(
        cotangent, mixed, CONTRACT_ROWS, preferred_element_type=jnp.float32
    )
    partial_grad = lax.psum_scatter(
        jnp.concatenate([first_term, second_term], axis=1), "fsdp", scatter_dimension=0, tiled=True
    )
    summed = lax.psum(partial_grad, "dp")
    norm_factor = 1.0 / math.sqrt(row_count * all_devices)
    grad_w_qkv = summed[:, : 3 * head_width] * norm_factor
    grad_w_out = summed[:, 3 * head_width :] * norm_factor
    return (output, grad_tokens, grad_w_qkv, grad_w_out)


MESH = pl.DeviceIdType.MESH
HEADS = 4
DIRECT = (0, 1)
HD = 128
PLAIN = (((1,), (0,)), ((), ()))


class Place:
    def __init__(self, fsdp_size):
        self.d, self.f = lax.axis_index("dp"), lax.axis_index("fsdp")
        self.c = lax.rem(self.d, 2)
        chip = lax.div(self.d, 2)
        self.x, self.y = lax.rem(chip, 2), lax.div(chip, 2)
        self.dx = self.dp_of(self.y, 1 - self.x, self.c)
        self.dy = self.dp_of(1 - self.y, self.x, self.c)
        self.dd = self.dp_of(1 - self.y, 1 - self.x, self.c)
        self.dc = self.dp_of(self.y, self.x, 1 - self.c)
        self.q = self.y * 2 + self.x
        self.qx = self.y * 2 + 1 - self.x
        self.qy = (1 - self.y) * 2 + self.x
        self.n = fsdp_size

    def dp_of(self, y, x, c):
        return (y * 2 + x) * 2 + c

    def ahead(self, j):
        return lax.rem(self.f + j, self.n)

    def behind(self, j):
        return lax.rem(self.f + self.n - j, self.n)

    def barrier(self):
        sem = pltpu.get_barrier_semaphore()
        targets = [(d, self.f) for d in (self.dx, self.dy, self.dd, self.dc)]
        targets += [(self.d, self.ahead(j)) for j in range(1, self.n)]
        for target in targets:
            pl.semaphore_signal(sem, inc=1, device_id=target, device_id_type=MESH)
        pl.semaphore_wait(sem, len(targets))


def dot(left, right, dims=PLAIN):
    return lax.dot_general(left, right, dims, preferred_element_type=jnp.float32)


def remote(src, dst, send_sem, recv_sem, target):
    return pltpu.make_async_remote_copy(
        src_ref=src,
        dst_ref=dst,
        send_sem=send_sem,
        recv_sem=recv_sem,
        device_id=target,
        device_id_type=MESH,
    )


def loop(count, work):
    def step(i, carry):
        work(i)
        return carry

    lax.fori_loop(0, count, step, 0)


def layer_kernel(
    n,
    tok_ref,
    cot_ref,
    wq_ref,
    wo_ref,
    doc_ref,
    sum_ref,
    out_ref,
    gt_ref,
    toks,
    cots,
    toks_t,
    cots_t,
    bias,
    w,
    x,
    g,
    grads,
    pair,
    plane,
    z_terms,
    part_out,
    part_in,
    result,
    sums,
    z_first,
    z_sum,
    pair_first,
    plane_first,
    g_send,
    g_recv,
    r_send,
    r_recv,
    c_send,
    c_recv,
    local_sem,
):
    me = Place(n)
    rows = toks.shape[1]
    wide = toks.shape[2]
    shard = wide // n
    quarter = shard // 4
    half = quarter // 2
    sub = 2 * HD
    last = HEADS - 1
    scale = HD ** (-0.5)

    def load_act(i):
        src, dst = ((tok_ref, toks), (cot_ref, cots))[i]
        return pltpu.make_async_copy(src, dst.at[0], local_sem.at[i])

    def load_w(k, p):
        src, base = (wq_ref, p * wo_ref.shape[1]) if p < 3 else (wo_ref, 0)
        first = pl.multiple_of(base + (me.c * HEADS + k) * HD, HD)
        spot = pl.ds(pl.multiple_of(me.f * shard, shard), shard)
        return pltpu.make_async_copy(
            src.at[:, pl.ds(first, HD)],
            w.at[k, spot, pl.ds(p * HD, HD)],
            local_sem.at[2 + k * 4 + p],
        )

    for k in range(HEADS):
        for p in range(4):
            load_w(k, p).start()
        if k < 2:
            load_act(k).start()
    me.barrier()

    def span(k, f, q, first, count):
        start = pl.multiple_of(f * shard + q * quarter + first, half)
        return w.at[k, pl.ds(start, count)]

    def gather(kind, k, j):
        f = me.f if kind == 0 else me.behind(j)
        q, first, count, target = (
            (me.q, 0, quarter, (me.d, me.ahead(j))),
            (me.q, 0, quarter, (me.dx, me.f)),
            (me.q, 0, quarter, (me.dy, me.f)),
            (me.qx, 0, half, (me.dy, me.f)),
            (me.qy, half, half, (me.dx, me.f)),
            (me.q, 0, quarter, (me.dd, me.f)),
        )[kind]
        spot = span(k, f, q, first, count)
        slot = (kind if kind < 5 else 3) * (n - 1) + j - 1
        return remote(spot, spot, g_send.at[k, slot], g_recv.at[k, slot], target)

    for k in range(HEADS):
        for p in range(4):
            load_w(k, p).wait()
        if k < 2:
            for j in range(1, n):
                gather(0, k, j).start()

    def from_z(k, j):
        gather(0, k, j).wait_recv()
        gather(1, k, j).start()
        gather(2, k, j).start()
        if k in DIRECT:
            gather(5, k, j).start()
        if k + 2 < HEADS:
            gather(0, k + 2, j).start()

    def from_plane(k, j):
        if k in DIRECT:
            return
        gather(1, k, j).wait_recv()
        gather(3, k, j).start()
        gather(2, k, j).wait_recv()
        gather(4, k, j).start()

    def relay_z(k):
        for j in range(1, n):
            from_z(k, j)

    def relay_plane(k):
        for j in range(1, n):
            from_plane(k, j)

    def gathered(k):
        for j in range(1, n):
            for kind in (1, 2, 5) if k in DIRECT else (3, 4):
                gather(kind, k, j).wait_recv()

    def cross(i):
        src, dst = (
            (toks.at[0], toks.at[1]),
            (cots.at[0], cots.at[1]),
            (bias.at[0], bias.at[1]),
            (part_out.at[0], part_in.at[0]),
            (part_out.at[1], part_in.at[1]),
        )[i]
        return remote(src, dst, c_send.at[i], c_recv.at[i], (me.dc, me.f))

    for i in range(2):
        load_act(i).wait()
        cross(i).start()

    block = rows // doc_ref.shape[1]
    key_row = lax.broadcasted_iota(jnp.int32, (rows, rows), 0)
    query_row = lax.broadcasted_iota(jnp.int32, (rows, rows), 1)

    def doc_of(row):
        ids = jnp.full(row.shape, doc_ref[0, 0], jnp.int32)
        for b in range(1, doc_ref.shape[1]):
            ids = jnp.where(row >= b * block, doc_ref[0, b], ids)
        return ids

    docs_k = doc_of(lax.broadcasted_iota(jnp.int32, (rows, HD), 0))
    docs_q = doc_of(lax.broadcasted_iota(jnp.int32, (8, rows), 1))
    same = docs_k[:, :1] == docs_q[:1, :]
    allowed = same & (key_row <= query_row)
    bias[0] = jnp.where(allowed, 0.0, NEG_FILL).astype(jnp.bfloat16)
    cross(2).start()

    def turn(s):
        def one(i):
            part = pl.ds(pl.multiple_of(i * HD, HD), HD)
            spot = pl.ds(s * rows, rows)
            toks_t[part, spot] = toks[s, :, part].T
            cots_t[part, spot] = cots[s, :, part].T

        loop(wide // HD, one)

    turn(0)
    for j in range(1, n + 1):
        if j < n:
            from_z(0, j)
        if j > 1:
            from_plane(0, j - 1)
    relay_z(1)

    def project(k, s):
        x[s, :, : 3 * HD] = dot(toks[s], w[k, :, : 3 * HD]).astype(jnp.bfloat16)
        x[s, :, 3 * HD :] = dot(cots[s], w[k, :, 3 * HD :]).astype(jnp.bfloat16)

    def attend(k, s):
        key, value = x[s, :, HD : 2 * HD], x[s, :, 2 * HD : 3 * HD]
        key_t, value_t = key.T, value.T
        grad_k, grad_v = None, None
        base = pl.multiple_of(s * rows, rows)
        for part in (1, 0):
            span_q = slice(part * rows // 2, (part + 1) * rows // 2)
            deep = (part + 1) * rows // 2
            query, gm = x[s, span_q, :HD], x[s, span_q, 3 * HD :]
            scores = dot(key[:deep], query, CONTRACT_COLS) * scale
            scores = scores + bias[s, :deep, span_q].astype(jnp.float32)
            expvals = jnp.exp(scores - jnp.max(scores, axis=0, keepdims=True))
            probs = expvals * (1.0 / jnp.sum(expvals, axis=0, keepdims=True))
            probs_half = probs.astype(jnp.bfloat16)
            mixed = dot(value_t[:, :deep], probs_half).astype(jnp.bfloat16)
            grad_probs = dot(value[:deep], gm, CONTRACT_COLS)
            inner = jnp.sum(probs * grad_probs, axis=0, keepdims=True)
            grad_scores = (probs * (grad_probs - inner)).astype(jnp.bfloat16)
            grad_q = (dot(key_t[:, :deep], grad_scores) * scale).astype(jnp.bfloat16)
            spot = pl.ds(base + part * (rows // 2), rows // 2)
            g[k, spot, :HD] = grad_q.T
            g[k, spot, 3 * HD :] = mixed.T
            more_k, more_v = dot(grad_scores, query), dot(probs_half, gm)
            if part == 1:
                grad_k, grad_v = more_k, more_v
            else:
                low = pl.ds(base, rows // 2)
                high = pl.ds(base + rows // 2, rows // 2)
                more_k, more_v = more_k + grad_k[:deep], more_v + grad_v[:deep]
                g[k, low, HD : 2 * HD] = (more_k * scale).astype(jnp.bfloat16)
                g[k, low, 2 * HD : 3 * HD] = more_v.astype(jnp.bfloat16)
                g[k, high, HD : 2 * HD] = (grad_k[deep:] * scale).astype(jnp.bfloat16)
                g[k, high, 2 * HD : 3 * HD] = grad_v[deep:].astype(jnp.bfloat16)

    def weight_grad(k, a):
        m = 2 * k + a

        def one(i):
            deep = 2 * shard
            spot = pl.ds(pl.multiple_of(i * deep, deep), deep)
            fs = pl.ds(2 * i, 2)
            if a == 0:
                total = dot(toks_t[spot, :], g[k, :, :sub]).astype(jnp.bfloat16)
                grads[m, fs] = total.reshape(2, 2, 2, quarter, sub)
            else:
                left = dot(toks_t[spot, :], g[k, :, sub : 3 * HD]).astype(jnp.bfloat16)
                right = dot(cots_t[spot, :], g[k, :, 3 * HD :]).astype(jnp.bfloat16)
                grads[m, fs, :, :, :, :HD] = left.reshape(2, 2, 2, quarter, HD)
                grads[m, fs, :, :, :, HD:] = right.reshape(2, 2, 2, quarter, HD)

        loop(n // 2, one)

    def columns_of(cut):
        return slice(None) if cut is None else pl.ds(cut * HD, HD)

    def reduce(kind, k, a, j=0, cut=None):
        m, cols = 2 * k + a, columns_of(cut)
        over_x, over_y = (me.dx, me.f), (me.dy, me.f)
        everything = pl.ds(0, quarter)
        if kind == 0:
            src = (
                grads.at[m, :, :, 1 - me.x, :, cols]
                if a == 0
                else grads.at[m, :, 1 - me.y, :, :, cols]
            )
            dst, target = pair.at[m, :, :, :, cols], over_x if a == 0 else over_y
        elif kind == 1:
            other = 1 - me.y if a == 0 else 1 - me.x
            src, dst = pair.at[m, :, other, :, cols], plane.at[m, :, :, cols]
            target = over_y if a == 0 else over_x
        elif kind == 2:
            src, dst = plane.at[m, me.ahead(j), :, cols], z_terms.at[m, j - 1, :, cols]
            target = (me.d, me.ahead(j))
        elif kind == 7:
            src, dst = sums.at[m, :, :, cols], sum_ref.at[me.c, m, :, :, cols]
            target = (me.dc, me.f)
        else:
            q, span_r, target = (
                (me.q, everything, over_x),
                (me.q, everything, over_y),
                (me.qx, pl.ds(0, half), over_y),
                (me.qy, pl.ds(half, half), over_x),
            )[kind - 3]
            src = sums.at[m, q, span_r, cols]
            dst = src
        slot = (kind if kind != 2 else 7 + j) + (0 if cut in (None, 0) else 7 + n)
        return remote(src, dst, r_send.at[m, slot], r_recv.at[m, slot], target)

    def first(kind, a, j=0):
        over_x, over_y = (me.dx, me.f), (me.dy, me.f)
        if kind == 0:
            src = z_sum.at[a, :, 1 - me.x] if a == 0 else z_sum.at[a, 1 - me.y]
            dst, target = pair_first.at[a], over_x if a == 0 else over_y
        elif kind == 1:
            src = pair_first.at[a, 1 - me.y] if a == 0 else pair_first.at[a, 1 - me.x]
            dst, target = plane_first.at[a], over_y if a == 0 else over_x
        else:
            src, dst = grads.at[a, me.ahead(j)], z_first.at[a, j - 1]
            target = (me.d, me.ahead(j))
        slot = kind if kind != 2 else 7 + j
        return remote(src, dst, r_send.at[a, slot], r_recv.at[a, slot], target)

    def first_z(a):
        for j in range(1, n):
            first(2, a, j).wait_recv()

        def one(i):
            y, x = lax.div(i, 2), lax.rem(i, 2)
            total = grads[a, me.f, y, x].astype(jnp.float32)
            for j in range(1, n):
                total = total + z_first[a, j - 1, y, x].astype(jnp.float32)
            z_sum[a, y, x] = total.astype(jnp.bfloat16)

        loop(4, one)
        first(0, a).start()

    def first_pair(a):
        first(0, a).wait_recv()
        for other in range(2):
            own = z_sum[a, other, me.x] if a == 0 else z_sum[a, me.y, other]
            pair_first[a, other] = add(own, pair_first[a, other])
        first(1, a).start()

    def first_plane(a):
        first(1, a).wait_recv()
        keep = me.y if a == 0 else me.x
        sums[a, me.q] = add(pair_first[a, keep], plane_first[a])
        reduce(3, 0, a).start()
        reduce(4, 0, a).start()

    def firsts(stage):
        stage(0)
        stage(1)

    def add(left, right):
        return left + right

    def stage_pair(k, a, cut=None):
        m, cols = 2 * k + a, columns_of(cut)
        reduce(0, k, a, 0, cut).wait_recv()

        def one(i):
            f, other = lax.div(i, 2), lax.rem(i, 2)
            y, x = (other, me.x) if a == 0 else (me.y, other)
            total = add(grads[m, f, y, x, :, cols], pair[m, f, other, :, cols])
            pair[m, f, other, :, cols] = total

        loop(2 * n, one)
        reduce(1, k, a, 0, cut).start()

    def stage_plane(k, a, cut=None):
        m, cols = 2 * k + a, columns_of(cut)
        reduce(1, k, a, 0, cut).wait_recv()
        stay = me.y if a == 0 else me.x

        def one(f):
            plane[m, f, :, cols] = add(pair[m, f, stay, :, cols], plane[m, f, :, cols])

        loop(n, one)
        for j in range(1, n):
            reduce(2, k, a, j, cut).start()

    def stage_z(k, a, cut=None):
        m, cols = 2 * k + a, columns_of(cut)
        total = plane[m, me.f, :, cols].astype(jnp.float32)
        for j in range(1, n):
            reduce(2, k, a, j, cut).wait_recv()
            total = total + z_terms[m, j - 1, :, cols].astype(jnp.float32)
        sums[m, me.q, :, cols] = total.astype(jnp.bfloat16)
        reduce(3, k, a, 0, cut).start()
        reduce(4, k, a, 0, cut).start()

    def stage_spread(k, a, cut=None):
        reduce(3, k, a, 0, cut).wait_recv()
        reduce(5, k, a, 0, cut).start()
        reduce(4, k, a, 0, cut).wait_recv()
        reduce(6, k, a, 0, cut).start()

    def stage_last(k, a, cut=None):
        reduce(5, k, a, 0, cut).wait_recv()
        reduce(6, k, a, 0, cut).wait_recv()
        reduce(7, k, a, 0, cut).start()
        if cut != 0:
            keep(2 * k + a).start()

    def keep(m):
        return pltpu.make_async_copy(sums.at[m], sum_ref.at[me.c, m], local_sem.at[2 + m])

    def both(stage, k, cut=None):
        stage(k, 0, cut)
        stage(k, 1, cut)

    def when(condition, *work):
        @pl.when(condition)
        def _():
            for one in work:
                one()

    def partner():
        for i in range(3):
            cross(i).wait_recv()
        turn(1)

    call = functools.partial

    def head(k):
        for one in range(HEADS):
            when(k == one, call(gathered, one))

        def sequence(s):
            when((k == 0) & (s == 1), partner)
            project(k, s)
            attend(k, s)
            when((k == 0) & (s == 0), call(relay_plane, 1))
            when((k == 0) & (s == 0), call(relay_z, 2))
            when((k == 1) & (s == 1), call(relay_plane, 3))

        loop(2, sequence)
        when(k > 2, call(both, stage_pair, k - 2))

        def columns(a):
            weight_grad(k, a)

            @pl.when(k == 0)
            def _():
                for j in range(1, n):
                    first(2, a, j).start()

            @pl.when((k > 0) & (k < last))
            def _():
                reduce(0, k, a).start()

        columns(0)
        columns(1)
        when(k == 0, call(relay_z, 3))
        when(k == 0, call(relay_plane, 2))

    loop(HEADS, head)
    for cut in range(2):
        for a in range(2):
            reduce(0, last, a, 0, cut).start()

    def product(which, s, i):
        cols = pl.ds(pl.multiple_of(i * sub, sub), sub)
        spot = pl.ds(s * rows, rows)
        part = slice(3 * HD, 4 * HD) if which == 0 else slice(0, 3 * HD)
        total = None
        for k in range(HEADS):
            more = dot(g[k, spot, part], w[k, cols, part], CONTRACT_COLS)
            total = more if total is None else total + more
        if s == 1:
            part_out[which, :, cols] = total.astype(jnp.bfloat16)
        else:
            total = total + part_in[which, :, cols].astype(jnp.float32)
            result[which, :, cols] = total.astype(jnp.bfloat16)

    def write(which):
        dst = (out_ref, gt_ref)[which]
        return pltpu.make_async_copy(result.at[which], dst, local_sem.at[which])

    def products(which, s):
        loop(wide // sub, functools.partial(product, which, s))

    both(stage_pair, 2)
    products(0, 1)
    cross(3).start()
    both(stage_plane, 1)
    firsts(first_z)
    both(stage_plane, 2)
    both(stage_pair, last, 0)
    both(stage_pair, last, 1)
    products(1, 1)
    cross(4).start()
    both(stage_z, 1)
    firsts(first_pair)
    both(stage_plane, last, 0)
    both(stage_plane, last, 1)
    both(stage_spread, 1)
    both(stage_z, 2)
    firsts(first_plane)
    both(stage_z, last, 0)
    both(stage_spread, 2)
    both(stage_z, last, 1)
    both(stage_spread, 0)
    cross(3).wait_recv()
    products(0, 0)
    write(0).start()
    both(stage_spread, last, 0)
    both(stage_last, 1)
    both(stage_spread, last, 1)
    cross(4).wait_recv()
    products(1, 0)
    write(1).start()
    both(stage_last, 2)
    both(stage_last, 0)
    both(stage_last, last, 0)
    both(stage_last, last, 1)

    def drain_gather(k):
        for kind in (0, 1, 2, 5) if k in DIRECT else range(5):
            for j in range(1, n):
                gather(kind, k, j).wait_send()

    def drain(k, cut=None, kinds=(0, 1, 3, 4, 5, 6, 7)):
        for a in range(2):
            for kind in kinds:
                reduce(kind, k, a, 0, cut).wait_send()
            if 0 in kinds:
                for j in range(1, n):
                    reduce(2, k, a, j, cut).wait_send()
            reduce(7, k, a, 0, cut).wait_recv()
            if cut != 0:
                keep(2 * k + a).wait()

    for k in range(HEADS):
        drain_gather(k)
    drain(0, None, (3, 4, 5, 6, 7))
    loop(last - 1, lambda i: drain(i + 1))
    drain(last, 0)
    drain(last, 1)
    for a in range(2):
        first(0, a).wait_send()
        first(1, a).wait_send()
        for j in range(1, n):
            first(2, a, j).wait_send()
    for which in range(2):
        write(which).wait()
    for i in range(5):
        cross(i).wait_send()


def layer(n, tokens, cotangent, w_qkv, w_out, doc_blocks):
    rows, wide = tokens.shape
    shard = wide // n
    quarter = shard // 4
    subs = 2 * HEADS
    anywhere = pl.BlockSpec(memory_space=pl.ANY)

    def room(*shape):
        return pltpu.VMEM(shape, jnp.bfloat16)

    dma = pltpu.SemaphoreType.DMA
    return pl.pallas_call(
        functools.partial(layer_kernel, n),
        out_shape=[
            jax.ShapeDtypeStruct((2, subs, 4, quarter, 2 * HD), jnp.bfloat16),
            jax.ShapeDtypeStruct((rows, wide), jnp.bfloat16),
            jax.ShapeDtypeStruct((rows, wide), jnp.bfloat16),
        ],
        in_specs=[anywhere] * 4 + [pl.BlockSpec(memory_space=pltpu.SMEM)],
        out_specs=[anywhere] * 3,
        scratch_shapes=[
            room(2, rows, wide),
            room(2, rows, wide),
            room(wide, 2 * rows),
            room(wide, 2 * rows),
            room(2, rows, rows),
            room(HEADS, wide, 4 * HD),
            room(2, rows, 4 * HD),
            room(HEADS, 2 * rows, 4 * HD),
            room(subs, n, 2, 2, quarter, 2 * HD),
            room(subs, n, 2, quarter, 2 * HD),
            room(subs, n, quarter, 2 * HD),
            room(subs, n - 1, quarter, 2 * HD),
            room(2, rows, wide),
            room(2, rows, wide),
            room(2, rows, wide),
            room(subs, 4, quarter, 2 * HD),
            room(2, n - 1, 2, 2, quarter, 2 * HD),
            room(2, 2, 2, quarter, 2 * HD),
            room(2, 2, quarter, 2 * HD),
            room(2, quarter, 2 * HD),
            dma((HEADS, 5 * (n - 1))),
            dma((HEADS, 5 * (n - 1))),
            dma((subs, 2 * (7 + n))),
            dma((subs, 2 * (7 + n))),
            dma((5,)),
            dma((5,)),
            dma((2 + 4 * HEADS,)),
        ],
        compiler_params=pltpu.CompilerParams(
            collective_id=0, has_side_effects=True, vmem_limit_bytes=56 << 20
        ),
        name="layer",
    )(tokens, cotangent, w_qkv, w_out, doc_blocks)


def finish_kernel(
    norm, sum_ref, out_in, gt_in, out_ref, gt_ref, gq_ref, go_ref, sums, acts, gq, go, load_sem, store_sem
):
    width, quarter = go.shape[1], sums.shape[3]

    def load(q):
        return pltpu.make_async_copy(sum_ref.at[:, :, q], sums.at[:, :, q], load_sem.at[q])

    def store(q, i):
        src, dst = ((gq, gq_ref), (go, go_ref))[i]
        span = pl.ds(q * quarter, quarter)
        return pltpu.make_async_copy(src.at[span], dst.at[span], store_sem.at[q, i])

    def act(i, leave):
        src, dst = ((out_in, out_ref), (gt_in, gt_ref))[i]
        if leave:
            return pltpu.make_async_copy(acts.at[i], dst, store_sem.at[4, i])
        return pltpu.make_async_copy(src, acts.at[i], load_sem.at[4 + i])

    for i in range(2):
        act(i, False).start()
    for q in range(4):
        load(q).start()
    for i in range(2):
        act(i, False).wait()
        act(i, True).start()

    for q in range(4):
        load(q).wait()
        span = pl.ds(q * quarter, quarter)
        for c in range(2):
            for m in range(2 * HEADS):
                head = c * HEADS + m // 2
                for i in range(2):
                    value = sums[c, m, q, :, i * HD : (i + 1) * HD].astype(jnp.float32) * norm
                    p = (m % 2) * 2 + i
                    if p < 3:
                        gq[span, p * width + head * HD : p * width + (head + 1) * HD] = value
                    else:
                        go[span, head * HD : (head + 1) * HD] = value
        for i in range(2):
            store(q, i).start()
    for q in range(4):
        for i in range(2):
            store(q, i).wait()
    for i in range(2):
        act(i, True).wait()


def finish(norm, sums, output, grad_tokens):
    rows, wide = output.shape
    quarter, width = sums.shape[3], 2 * HEADS * HD
    anywhere = pl.BlockSpec(memory_space=pl.ANY)
    grads = [(4 * quarter, 3 * width), (4 * quarter, width)]
    return pl.pallas_call(
        functools.partial(finish_kernel, norm),
        out_shape=[jax.ShapeDtypeStruct((rows, wide), jnp.bfloat16)] * 2
        + [jax.ShapeDtypeStruct(shape, jnp.float32) for shape in grads],
        in_specs=[anywhere] * 3,
        out_specs=[anywhere] * 4,
        scratch_shapes=[pltpu.VMEM(shape, jnp.bfloat16) for shape in (sums.shape, (2, rows, wide))]
        + [pltpu.VMEM(shape, jnp.float32) for shape in grads]
        + [pltpu.SemaphoreType.DMA((6,)), pltpu.SemaphoreType.DMA((5, 2))],
        compiler_params=pltpu.CompilerParams(vmem_limit_bytes=60 << 20),
        name="finish",
    )(sums, output, grad_tokens)


def chip_body(tokens, w_qkv, w_out, doc_blocks, cotangent):
    n = lax.axis_size("fsdp")
    all_devices = lax.axis_size("dp") * n
    sums, output, grad_tokens = layer(n, tokens, cotangent, w_qkv, w_out, doc_blocks)
    norm_factor = 1.0 / math.sqrt(tokens.shape[0] * all_devices)
    return tuple(finish(norm_factor, sums, output, grad_tokens))


def solution(mesh):
    placed = (
        P(("dp", "fsdp"), None),
        P("fsdp", None),
        P("fsdp", None),
        P(("dp", "fsdp"), None),
        P(("dp", "fsdp"), None),
    )
    in_plane = mesh.shape["dp"] == 8 and mesh.shape["fsdp"] == 4
    return jax.shard_map(
        chip_body if in_plane else body,
        mesh=mesh,
        in_specs=placed,
        out_specs=(
            P(("dp", "fsdp"), None),
            P(("dp", "fsdp"), None),
            P("fsdp", None),
            P("fsdp", None),
        ),
        check_vma=False,
    )
```

```python
import functools
import math

import jax
import jax.numpy as jnp
from jax import lax
from jax.experimental import pallas as pl
from jax.experimental.pallas import tpu as pltpu
from jax.sharding import PartitionSpec as P

H = 8


NEG_FILL = -1e30
CONTRACT_ROWS = (((0,), (0,)), ((), ()))
CONTRACT_COLS = (((1,), (1,)), ((), ()))


def row_mask(doc_ids, row_count):
    block_len = row_count // doc_ids.shape[0]
    doc_rows = jnp.repeat(doc_ids, block_len, total_repeat_length=row_count)
    position = jnp.arange(row_count, dtype=jnp.int32)
    causal = position[None, :] <= position[:, None]
    return causal & (doc_rows[None, :] == doc_rows[:, None])


def split_heads(matrix, head_count):
    return matrix.reshape(matrix.shape[0], head_count, matrix.shape[1] // head_count)


def attend_forward(query_rows, key_rows, value_rows, allowed, head_count):
    row_count = query_rows.shape[0]
    query_heads = split_heads(query_rows, head_count)
    key_heads = split_heads(key_rows, head_count)
    value_heads = split_heads(value_rows, head_count)
    score_scale = query_heads.shape[2] ** (-0.5)
    scores = (
        jnp.einsum("qhd,khd->hqk", query_heads, key_heads, preferred_element_type=jnp.float32)
        * score_scale
    )
    scores = jnp.where(allowed[None], scores, NEG_FILL)
    highest = jnp.max(scores, axis=-1, keepdims=True)
    expvals = jnp.exp(scores - highest)
    attn_probs = expvals / jnp.sum(expvals, axis=-1, keepdims=True)
    probs_half = attn_probs.astype(jnp.bfloat16)
    mixed = jnp.einsum("hqk,khd->qhd", probs_half, value_heads, preferred_element_type=jnp.float32)
    return (mixed.astype(jnp.bfloat16).reshape(row_count, -1), attn_probs, probs_half)


def attend_backward(
    query_rows, key_rows, value_rows, attn_probs, probs_half, grad_mixed, head_count
):
    row_count = query_rows.shape[0]
    query_heads = split_heads(query_rows, head_count)
    key_heads = split_heads(key_rows, head_count)
    value_heads = split_heads(value_rows, head_count)
    grad_heads = split_heads(grad_mixed, head_count)
    score_scale = query_heads.shape[2] ** (-0.5)
    grad_probs = jnp.einsum(
        "qhd,khd->hqk", grad_heads, value_heads, preferred_element_type=jnp.float32
    )
    grad_values = jnp.einsum(
        "hqk,qhd->khd", probs_half, grad_heads, preferred_element_type=jnp.float32
    )
    inner = jnp.sum(attn_probs * grad_probs, axis=-1, keepdims=True)
    grad_scores = (attn_probs * (grad_probs - inner)).astype(jnp.bfloat16)
    grad_queries = (
        jnp.einsum("hqk,khd->qhd", grad_scores, key_heads, preferred_element_type=jnp.float32)
        * score_scale
    )
    grad_keys = (
        jnp.einsum("hqk,qhd->khd", grad_scores, query_heads, preferred_element_type=jnp.float32)
        * score_scale
    )
    pieces_list = [grad_queries, grad_keys, grad_values]
    return jnp.concatenate(
        [p.astype(jnp.bfloat16).reshape(row_count, -1) for p in pieces_list], axis=1
    )


def body(tokens, w_qkv, w_out, doc_blocks, cotangent):
    row_count = tokens.shape[0]
    head_width = w_out.shape[1]
    head_count = H
    all_devices = lax.axis_size("dp") * lax.axis_size("fsdp")
    allowed = row_mask(doc_blocks[0], row_count)
    columns = tokens
    qkv = jnp.dot(
        columns,
        lax.all_gather(w_qkv, "fsdp", axis=0, tiled=True),
        preferred_element_type=jnp.float32,
    ).astype(jnp.bfloat16)
    query_rows = qkv[:, :head_width]
    key_rows = qkv[:, head_width : 2 * head_width]
    value_rows = qkv[:, 2 * head_width :]
    mixed, attn_probs, probs_half = attend_forward(
        query_rows, key_rows, value_rows, allowed, head_count
    )
    output = lax.dot_general(
        mixed,
        lax.all_gather(w_out, "fsdp", axis=0, tiled=True),
        CONTRACT_COLS,
        preferred_element_type=jnp.float32,
    )
    columns = cotangent
    grad_mixed = jnp.dot(
        columns,
        lax.all_gather(w_out, "fsdp", axis=0, tiled=True),
        preferred_element_type=jnp.float32,
    ).astype(jnp.bfloat16)
    output = output.astype(jnp.bfloat16)
    grad_qkv = attend_backward(
        query_rows, key_rows, value_rows, attn_probs, probs_half, grad_mixed, head_count
    )
    grad_tokens = lax.dot_general(
        grad_qkv,
        lax.all_gather(w_qkv, "fsdp", axis=0, tiled=True),
        CONTRACT_COLS,
        preferred_element_type=jnp.float32,
    )
    grad_tokens = grad_tokens.astype(jnp.bfloat16)
    first_term = lax.dot_general(
        tokens, grad_qkv, CONTRACT_ROWS, preferred_element_type=jnp.float32
    )
    second_term = lax.dot_general(
        cotangent, mixed, CONTRACT_ROWS, preferred_element_type=jnp.float32
    )
    partial_grad = lax.psum_scatter(
        jnp.concatenate([first_term, second_term], axis=1), "fsdp", scatter_dimension=0, tiled=True
    )
    summed = lax.psum(partial_grad, "dp")
    norm_factor = 1.0 / math.sqrt(row_count * all_devices)
    grad_w_qkv = summed[:, : 3 * head_width] * norm_factor
    grad_w_out = summed[:, 3 * head_width :] * norm_factor
    return (output, grad_tokens, grad_w_qkv, grad_w_out)


MESH = pl.DeviceIdType.MESH
HEADS = 4
DIRECT = (0, 1)
HD = 128
PLAIN = (((1,), (0,)), ((), ()))


class Place:
    def __init__(self, fsdp_size):
        self.d, self.f = lax.axis_index("dp"), lax.axis_index("fsdp")
        self.c = lax.rem(self.d, 2)
        chip = lax.div(self.d, 2)
        self.x, self.y = lax.rem(chip, 2), lax.div(chip, 2)
        self.dx = self.dp_of(self.y, 1 - self.x, self.c)
        self.dy = self.dp_of(1 - self.y, self.x, self.c)
        self.dd = self.dp_of(1 - self.y, 1 - self.x, self.c)
        self.dc = self.dp_of(self.y, self.x, 1 - self.c)
        self.q = self.y * 2 + self.x
        self.qx = self.y * 2 + 1 - self.x
        self.qy = (1 - self.y) * 2 + self.x
        self.n = fsdp_size

    def dp_of(self, y, x, c):
        return (y * 2 + x) * 2 + c

    def ahead(self, j):
        return lax.rem(self.f + j, self.n)

    def behind(self, j):
        return lax.rem(self.f + self.n - j, self.n)

    def barrier(self):
        sem = pltpu.get_barrier_semaphore()
        targets = [(d, self.f) for d in (self.dx, self.dy, self.dd, self.dc)]
        targets += [(self.d, self.ahead(j)) for j in range(1, self.n)]
        for target in targets:
            pl.semaphore_signal(sem, inc=1, device_id=target, device_id_type=MESH)
        pl.semaphore_wait(sem, len(targets))


def dot(left, right, dims=PLAIN):
    return lax.dot_general(left, right, dims, preferred_element_type=jnp.float32)


def remote(src, dst, send_sem, recv_sem, target):
    return pltpu.make_async_remote_copy(
        src_ref=src,
        dst_ref=dst,
        send_sem=send_sem,
        recv_sem=recv_sem,
        device_id=target,
        device_id_type=MESH,
    )


def loop(count, work):
    def step(i, carry):
        work(i)
        return carry

    lax.fori_loop(0, count, step, 0)


def layer_kernel(
    n,
    tok_ref,
    cot_ref,
    wq_ref,
    wo_ref,
    doc_ref,
    sum_ref,
    out_ref,
    gt_ref,
    toks,
    cots,
    toks_t,
    cots_t,
    bias,
    w,
    x,
    g,
    grads,
    pair,
    plane,
    z_terms,
    part_out,
    part_in,
    result,
    sums,
    z_first,
    z_sum,
    pair_first,
    plane_first,
    g_send,
    g_recv,
    r_send,
    r_recv,
    c_send,
    c_recv,
    local_sem,
):
    me = Place(n)
    rows = toks.shape[1]
    wide = toks.shape[2]
    shard = wide // n
    quarter = shard // 4
    half = quarter // 2
    sub = 2 * HD
    last = HEADS - 1
    scale = HD ** (-0.5)

    def load_act(i):
        src, dst = ((tok_ref, toks), (cot_ref, cots))[i]
        return pltpu.make_async_copy(src, dst.at[0], local_sem.at[i])

    def load_w(k, p):
        src, base = (wq_ref, p * wo_ref.shape[1]) if p < 3 else (wo_ref, 0)
        first = pl.multiple_of(base + (me.c * HEADS + k) * HD, HD)
        spot = pl.ds(pl.multiple_of(me.f * shard, shard), shard)
        return pltpu.make_async_copy(
            src.at[:, pl.ds(first, HD)],
            w.at[k, spot, pl.ds(p * HD, HD)],
            local_sem.at[2 + k * 4 + p],
        )

    for k in range(HEADS):
        for p in range(4):
            load_w(k, p).start()
        if k < 2:
            load_act(k).start()
    me.barrier()

    def span(k, f, q, first, count):
        start = pl.multiple_of(f * shard + q * quarter + first, half)
        return w.at[k, pl.ds(start, count)]

    def gather(kind, k, j):
        f = me.f if kind == 0 else me.behind(j)
        q, first, count, target = (
            (me.q, 0, quarter, (me.d, me.ahead(j))),
            (me.q, 0, quarter, (me.dx, me.f)),
            (me.q, 0, quarter, (me.dy, me.f)),
            (me.qx, 0, half, (me.dy, me.f)),
            (me.qy, half, half, (me.dx, me.f)),
            (me.q, 0, quarter, (me.dd, me.f)),
        )[kind]
        spot = span(k, f, q, first, count)
        slot = (kind if kind < 5 else 3) * (n - 1) + j - 1
        return remote(spot, spot, g_send.at[k, slot], g_recv.at[k, slot], target)

    for k in range(HEADS):
        for p in range(4):
            load_w(k, p).wait()
        if k < 2:
            for j in range(1, n):
                gather(0, k, j).start()

    def from_z(k, j):
        gather(0, k, j).wait_recv()
        gather(1, k, j).start()
        gather(2, k, j).start()
        if k in DIRECT:
            gather(5, k, j).start()
        if k + 2 < HEADS:
            gather(0, k + 2, j).start()

    def from_plane(k, j):
        if k in DIRECT:
            return
        gather(1, k, j).wait_recv()
        gather(3, k, j).start()
        gather(2, k, j).wait_recv()
        gather(4, k, j).start()

    def relay_z(k):
        for j in range(1, n):
            from_z(k, j)

    def relay_plane(k):
        for j in range(1, n):
            from_plane(k, j)

    def gathered(k):
        for j in range(1, n):
            for kind in (1, 2, 5) if k in DIRECT else (3, 4):
                gather(kind, k, j).wait_recv()

    def cross(i):
        src, dst = (
            (toks.at[0], toks.at[1]),
            (cots.at[0], cots.at[1]),
            (bias.at[0], bias.at[1]),
            (part_out.at[0], part_in.at[0]),
            (part_out.at[1], part_in.at[1]),
        )[i]
        return remote(src, dst, c_send.at[i], c_recv.at[i], (me.dc, me.f))

    for i in range(2):
        load_act(i).wait()
        cross(i).start()

    block = rows // doc_ref.shape[1]
    key_row = lax.broadcasted_iota(jnp.int32, (rows, rows), 0)
    query_row = lax.broadcasted_iota(jnp.int32, (rows, rows), 1)

    def doc_of(row):
        ids = jnp.full(row.shape, doc_ref[0, 0], jnp.int32)
        for b in range(1, doc_ref.shape[1]):
            ids = jnp.where(row >= b * block, doc_ref[0, b], ids)
        return ids

    docs_k = doc_of(lax.broadcasted_iota(jnp.int32, (rows, HD), 0))
    docs_q = doc_of(lax.broadcasted_iota(jnp.int32, (8, rows), 1))
    same = docs_k[:, :1] == docs_q[:1, :]
    allowed = same & (key_row <= query_row)
    bias[0] = jnp.where(allowed, 0.0, NEG_FILL).astype(jnp.bfloat16)
    cross(2).start()

    def turn(s):
        def one(i):
            part = pl.ds(pl.multiple_of(i * HD, HD), HD)
            spot = pl.ds(s * rows, rows)
            toks_t[part, spot] = toks[s, :, part].T
            cots_t[part, spot] = cots[s, :, part].T

        loop(wide // HD, one)

    turn(0)
    for j in range(1, n + 1):
        if j < n:
            from_z(0, j)
        if j > 1:
            from_plane(0, j - 1)
    relay_z(1)

    def project(k, s):
        x[s, :, : 3 * HD] = dot(toks[s], w[k, :, : 3 * HD]).astype(jnp.bfloat16)
        x[s, :, 3 * HD :] = dot(cots[s], w[k, :, 3 * HD :]).astype(jnp.bfloat16)

    def attend(k, s):
        key, value = x[s, :, HD : 2 * HD], x[s, :, 2 * HD : 3 * HD]
        key_t, value_t = key.T, value.T
        grad_k, grad_v = None, None
        base = pl.multiple_of(s * rows, rows)
        for part in (1, 0):
            span_q = slice(part * rows // 2, (part + 1) * rows // 2)
            deep = (part + 1) * rows // 2
            query, gm = x[s, span_q, :HD], x[s, span_q, 3 * HD :]
            scores = dot(key[:deep], query, CONTRACT_COLS) * scale
            scores = scores + bias[s, :deep, span_q].astype(jnp.float32)
            expvals = jnp.exp(scores - jnp.max(scores, axis=0, keepdims=True))
            probs = expvals * (1.0 / jnp.sum(expvals, axis=0, keepdims=True))
            probs_half = probs.astype(jnp.bfloat16)
            mixed = dot(value_t[:, :deep], probs_half).astype(jnp.bfloat16)
            grad_probs = dot(value[:deep], gm, CONTRACT_COLS)
            inner = jnp.sum(probs * grad_probs, axis=0, keepdims=True)
            grad_scores = (probs * (grad_probs - inner)).astype(jnp.bfloat16)
            grad_q = (dot(key_t[:, :deep], grad_scores) * scale).astype(jnp.bfloat16)
            spot = pl.ds(base + part * (rows // 2), rows // 2)
            g[k, spot, :HD] = grad_q.T
            g[k, spot, 3 * HD :] = mixed.T
            more_k, more_v = dot(grad_scores, query), dot(probs_half, gm)
            if part == 1:
                grad_k, grad_v = more_k, more_v
            else:
                low = pl.ds(base, rows // 2)
                high = pl.ds(base + rows // 2, rows // 2)
                more_k, more_v = more_k + grad_k[:deep], more_v + grad_v[:deep]
                g[k, low, HD : 2 * HD] = (more_k * scale).astype(jnp.bfloat16)
                g[k, low, 2 * HD : 3 * HD] = more_v.astype(jnp.bfloat16)
                g[k, high, HD : 2 * HD] = (grad_k[deep:] * scale).astype(jnp.bfloat16)
                g[k, high, 2 * HD : 3 * HD] = grad_v[deep:].astype(jnp.bfloat16)

    def weight_grad(k, a):
        m = 2 * k + a

        def one(i):
            deep = 2 * shard
            spot = pl.ds(pl.multiple_of(i * deep, deep), deep)
            fs = pl.ds(2 * i, 2)
            if a == 0:
                total = dot(toks_t[spot, :], g[k, :, :sub]).astype(jnp.bfloat16)
                grads[m, fs] = total.reshape(2, 2, 2, quarter, sub)
            else:
                left = dot(toks_t[spot, :], g[k, :, sub : 3 * HD]).astype(jnp.bfloat16)
                right = dot(cots_t[spot, :], g[k, :, 3 * HD :]).astype(jnp.bfloat16)
                grads[m, fs, :, :, :, :HD] = left.reshape(2, 2, 2, quarter, HD)
                grads[m, fs, :, :, :, HD:] = right.reshape(2, 2, 2, quarter, HD)

        loop(n // 2, one)

    def columns_of(cut):
        return slice(None) if cut is None else pl.ds(cut * HD, HD)

    def reduce(kind, k, a, j=0, cut=None):
        m, cols = 2 * k + a, columns_of(cut)
        over_x, over_y = (me.dx, me.f), (me.dy, me.f)
        everything = pl.ds(0, quarter)
        if kind == 0:
            src = (
                grads.at[m, :, :, 1 - me.x, :, cols]
                if a == 0
                else grads.at[m, :, 1 - me.y, :, :, cols]
            )
            dst, target = pair.at[m, :, :, :, cols], over_x if a == 0 else over_y
        elif kind == 1:
            other = 1 - me.y if a == 0 else 1 - me.x
            src, dst = pair.at[m, :, other, :, cols], plane.at[m, :, :, cols]
            target = over_y if a == 0 else over_x
        elif kind == 2:
            src, dst = plane.at[m, me.ahead(j), :, cols], z_terms.at[m, j - 1, :, cols]
            target = (me.d, me.ahead(j))
        elif kind == 5 and cut is not None:
            src = sums.at[m, me.q, :, cols]
            dst, target = src, (me.dd, me.f)
        elif kind == 7:
            src, dst = sums.at[m, :, :, cols], sum_ref.at[me.c, m, :, :, cols]
            target = (me.dc, me.f)
        else:
            q, span_r, target = (
                (me.q, everything, over_x),
                (me.q, everything, over_y),
                (me.qx, pl.ds(0, half), over_y),
                (me.qy, pl.ds(half, half), over_x),
            )[kind - 3]
            src = sums.at[m, q, span_r, cols]
            dst = src
        slot = (kind if kind != 2 else 7 + j) + (0 if cut in (None, 0) else 7 + n)
        return remote(src, dst, r_send.at[m, slot], r_recv.at[m, slot], target)

    def first(kind, a, j=0):
        over_x, over_y = (me.dx, me.f), (me.dy, me.f)
        if kind == 0:
            src = z_sum.at[a, :, 1 - me.x] if a == 0 else z_sum.at[a, 1 - me.y]
            dst, target = pair_first.at[a], over_x if a == 0 else over_y
        elif kind == 1:
            src = pair_first.at[a, 1 - me.y] if a == 0 else pair_first.at[a, 1 - me.x]
            dst, target = plane_first.at[a], over_y if a == 0 else over_x
        else:
            src, dst = grads.at[a, me.ahead(j)], z_first.at[a, j - 1]
            target = (me.d, me.ahead(j))
        slot = kind if kind != 2 else 7 + j
        return remote(src, dst, r_send.at[a, slot], r_recv.at[a, slot], target)

    def first_z(a):
        for j in range(1, n):
            first(2, a, j).wait_recv()

        def one(i):
            y, x = lax.div(i, 2), lax.rem(i, 2)
            total = grads[a, me.f, y, x].astype(jnp.float32)
            for j in range(1, n):
                total = total + z_first[a, j - 1, y, x].astype(jnp.float32)
            z_sum[a, y, x] = total.astype(jnp.bfloat16)

        loop(4, one)
        first(0, a).start()

    def first_pair(a):
        first(0, a).wait_recv()
        for other in range(2):
            own = z_sum[a, other, me.x] if a == 0 else z_sum[a, me.y, other]
            pair_first[a, other] = add(own, pair_first[a, other])
        first(1, a).start()

    def first_plane(a):
        first(1, a).wait_recv()
        keep = me.y if a == 0 else me.x
        sums[a, me.q] = add(pair_first[a, keep], plane_first[a])
        reduce(3, 0, a).start()
        reduce(4, 0, a).start()

    def firsts(stage):
        stage(0)
        stage(1)

    def add(left, right):
        return left + right

    def stage_pair(k, a, cut=None):
        m, cols = 2 * k + a, columns_of(cut)
        reduce(0, k, a, 0, cut).wait_recv()

        def one(i):
            f, other = lax.div(i, 2), lax.rem(i, 2)
            y, x = (other, me.x) if a == 0 else (me.y, other)
            total = add(grads[m, f, y, x, :, cols], pair[m, f, other, :, cols])
            pair[m, f, other, :, cols] = total

        loop(2 * n, one)
        reduce(1, k, a, 0, cut).start()

    def stage_plane(k, a, cut=None):
        m, cols = 2 * k + a, columns_of(cut)
        reduce(1, k, a, 0, cut).wait_recv()
        stay = me.y if a == 0 else me.x

        def one(f):
            plane[m, f, :, cols] = add(pair[m, f, stay, :, cols], plane[m, f, :, cols])

        loop(n, one)
        for j in range(1, n):
            reduce(2, k, a, j, cut).start()

    def stage_z(k, a, cut=None):
        m, cols = 2 * k + a, columns_of(cut)
        total = plane[m, me.f, :, cols].astype(jnp.float32)
        for j in range(1, n):
            reduce(2, k, a, j, cut).wait_recv()
            total = total + z_terms[m, j - 1, :, cols].astype(jnp.float32)
        sums[m, me.q, :, cols] = total.astype(jnp.bfloat16)
        reduce(3, k, a, 0, cut).start()
        reduce(4, k, a, 0, cut).start()
        if cut is not None:
            reduce(5, k, a, 0, cut).start()

    def stage_spread(k, a, cut=None):
        reduce(3, k, a, 0, cut).wait_recv()
        reduce(5, k, a, 0, cut).start()
        reduce(4, k, a, 0, cut).wait_recv()
        reduce(6, k, a, 0, cut).start()

    def stage_last(k, a, cut=None):
        for kind in (5, 6) if cut is None else (3, 4, 5):
            reduce(kind, k, a, 0, cut).wait_recv()
        reduce(7, k, a, 0, cut).start()
        if cut != 0:
            keep(2 * k + a).start()

    def keep(m):
        return pltpu.make_async_copy(sums.at[m], sum_ref.at[me.c, m], local_sem.at[2 + m])

    def both(stage, k, cut=None):
        stage(k, 0, cut)
        stage(k, 1, cut)

    def when(condition, *work):
        @pl.when(condition)
        def _():
            for one in work:
                one()

    def partner():
        for i in range(3):
            cross(i).wait_recv()
        turn(1)

    call = functools.partial

    def head(k):
        for one in range(HEADS):
            when(k == one, call(gathered, one))

        def sequence(s):
            when((k == 0) & (s == 1), partner)
            project(k, s)
            attend(k, s)
            when((k == 0) & (s == 0), call(relay_plane, 1))
            when((k == 0) & (s == 0), call(relay_z, 2))
            when((k == 1) & (s == 1), call(relay_plane, 3))

        loop(2, sequence)
        when(k > 2, call(both, stage_pair, k - 2))

        def columns(a):
            weight_grad(k, a)

            @pl.when(k == 0)
            def _():
                for j in range(1, n):
                    first(2, a, j).start()

            @pl.when((k > 0) & (k < last))
            def _():
                reduce(0, k, a).start()

        columns(0)
        columns(1)
        when(k == 0, call(relay_z, 3))
        when(k == 0, call(relay_plane, 2))

    loop(HEADS, head)
    for cut in range(2):
        for a in range(2):
            reduce(0, last, a, 0, cut).start()

    def product(which, s, i):
        cols = pl.ds(pl.multiple_of(i * sub, sub), sub)
        spot = pl.ds(s * rows, rows)
        part = slice(3 * HD, 4 * HD) if which == 0 else slice(0, 3 * HD)
        total = None
        for k in range(HEADS):
            more = dot(g[k, spot, part], w[k, cols, part], CONTRACT_COLS)
            total = more if total is None else total + more
        if s == 1:
            part_out[which, :, cols] = total.astype(jnp.bfloat16)
        else:
            total = total + part_in[which, :, cols].astype(jnp.float32)
            result[which, :, cols] = total.astype(jnp.bfloat16)

    def write(which):
        dst = (out_ref, gt_ref)[which]
        return pltpu.make_async_copy(result.at[which], dst, local_sem.at[which])

    def products(which, s):
        loop(wide // sub, functools.partial(product, which, s))

    both(stage_pair, 2)
    products(0, 1)
    cross(3).start()
    both(stage_plane, 1)
    firsts(first_z)
    both(stage_plane, 2)
    both(stage_pair, last, 0)
    both(stage_pair, last, 1)
    products(1, 1)
    cross(4).start()
    both(stage_z, 1)
    firsts(first_pair)
    both(stage_plane, last, 0)
    both(stage_plane, last, 1)
    both(stage_spread, 1)
    both(stage_z, 2)
    firsts(first_plane)
    both(stage_z, last, 0)
    both(stage_spread, 2)
    both(stage_z, last, 1)
    both(stage_spread, 0)
    cross(3).wait_recv()
    products(0, 0)
    write(0).start()
    both(stage_last, 1)
    cross(4).wait_recv()
    products(1, 0)
    write(1).start()
    both(stage_last, 2)
    both(stage_last, 0)
    both(stage_last, last, 0)
    both(stage_last, last, 1)

    def drain_gather(k):
        for kind in (0, 1, 2, 5) if k in DIRECT else range(5):
            for j in range(1, n):
                gather(kind, k, j).wait_send()

    def drain(k, cut=None, kinds=(0, 1, 3, 4, 5, 6, 7)):
        for a in range(2):
            for kind in kinds:
                reduce(kind, k, a, 0, cut).wait_send()
            if 0 in kinds:
                for j in range(1, n):
                    reduce(2, k, a, j, cut).wait_send()
            reduce(7, k, a, 0, cut).wait_recv()
            if cut != 0:
                keep(2 * k + a).wait()

    for k in range(HEADS):
        drain_gather(k)
    drain(0, None, (3, 4, 5, 6, 7))
    loop(last - 1, lambda i: drain(i + 1))
    for cut in range(2):
        drain(last, cut, (0, 1, 3, 4, 5, 7))
    for a in range(2):
        first(0, a).wait_send()
        first(1, a).wait_send()
        for j in range(1, n):
            first(2, a, j).wait_send()
    for which in range(2):
        write(which).wait()
    for i in range(5):
        cross(i).wait_send()


def layer(n, tokens, cotangent, w_qkv, w_out, doc_blocks):
    rows, wide = tokens.shape
    shard = wide // n
    quarter = shard // 4
    subs = 2 * HEADS
    anywhere = pl.BlockSpec(memory_space=pl.ANY)

    def room(*shape):
        return pltpu.VMEM(shape, jnp.bfloat16)

    dma = pltpu.SemaphoreType.DMA
    return pl.pallas_call(
        functools.partial(layer_kernel, n),
        out_shape=[
            jax.ShapeDtypeStruct((2, subs, 4, quarter, 2 * HD), jnp.bfloat16),
            jax.ShapeDtypeStruct((rows, wide), jnp.bfloat16),
            jax.ShapeDtypeStruct((rows, wide), jnp.bfloat16),
        ],
        in_specs=[anywhere] * 4 + [pl.BlockSpec(memory_space=pltpu.SMEM)],
        out_specs=[anywhere] * 3,
        scratch_shapes=[
            room(2, rows, wide),
            room(2, rows, wide),
            room(wide, 2 * rows),
            room(wide, 2 * rows),
            room(2, rows, rows),
            room(HEADS, wide, 4 * HD),
            room(2, rows, 4 * HD),
            room(HEADS, 2 * rows, 4 * HD),
            room(subs, n, 2, 2, quarter, 2 * HD),
            room(subs, n, 2, quarter, 2 * HD),
            room(subs, n, quarter, 2 * HD),
            room(subs, n - 1, quarter, 2 * HD),
            room(2, rows, wide),
            room(2, rows, wide),
            room(2, rows, wide),
            room(subs, 4, quarter, 2 * HD),
            room(2, n - 1, 2, 2, quarter, 2 * HD),
            room(2, 2, 2, quarter, 2 * HD),
            room(2, 2, quarter, 2 * HD),
            room(2, quarter, 2 * HD),
            dma((HEADS, 5 * (n - 1))),
            dma((HEADS, 5 * (n - 1))),
            dma((subs, 2 * (7 + n))),
            dma((subs, 2 * (7 + n))),
            dma((5,)),
            dma((5,)),
            dma((2 + 4 * HEADS,)),
        ],
        compiler_params=pltpu.CompilerParams(
            collective_id=0, has_side_effects=True, vmem_limit_bytes=56 << 20
        ),
        name="layer",
    )(tokens, cotangent, w_qkv, w_out, doc_blocks)


def finish_kernel(
    norm, sum_ref, out_in, gt_in, out_ref, gt_ref, gq_ref, go_ref, sums, acts, gq, go, load_sem, store_sem
):
    width, quarter = go.shape[1], sums.shape[3]

    def load(q):
        return pltpu.make_async_copy(sum_ref.at[:, :, q], sums.at[:, :, q], load_sem.at[q])

    def store(q, i):
        src, dst = ((gq, gq_ref), (go, go_ref))[i]
        span = pl.ds(q * quarter, quarter)
        return pltpu.make_async_copy(src.at[span], dst.at[span], store_sem.at[q, i])

    def act(i, leave):
        src, dst = ((out_in, out_ref), (gt_in, gt_ref))[i]
        if leave:
            return pltpu.make_async_copy(acts.at[i], dst, store_sem.at[4, i])
        return pltpu.make_async_copy(src, acts.at[i], load_sem.at[4 + i])

    for i in range(2):
        act(i, False).start()
    for q in range(4):
        load(q).start()
    for i in range(2):
        act(i, False).wait()
        act(i, True).start()

    for q in range(4):
        load(q).wait()
        span = pl.ds(q * quarter, quarter)
        for c in range(2):
            for m in range(2 * HEADS):
                head = c * HEADS + m // 2
                for i in range(2):
                    value = sums[c, m, q, :, i * HD : (i + 1) * HD].astype(jnp.float32) * norm
                    p = (m % 2) * 2 + i
                    if p < 3:
                        gq[span, p * width + head * HD : p * width + (head + 1) * HD] = value
                    else:
                        go[span, head * HD : (head + 1) * HD] = value
        for i in range(2):
            store(q, i).start()
    for q in range(4):
        for i in range(2):
            store(q, i).wait()
    for i in range(2):
        act(i, True).wait()


def finish(norm, sums, output, grad_tokens):
    rows, wide = output.shape
    quarter, width = sums.shape[3], 2 * HEADS * HD
    anywhere = pl.BlockSpec(memory_space=pl.ANY)
    grads = [(4 * quarter, 3 * width), (4 * quarter, width)]
    return pl.pallas_call(
        functools.partial(finish_kernel, norm),
        out_shape=[jax.ShapeDtypeStruct((rows, wide), jnp.bfloat16)] * 2
        + [jax.ShapeDtypeStruct(shape, jnp.float32) for shape in grads],
        in_specs=[anywhere] * 3,
        out_specs=[anywhere] * 4,
        scratch_shapes=[pltpu.VMEM(shape, jnp.bfloat16) for shape in (sums.shape, (2, rows, wide))]
        + [pltpu.VMEM(shape, jnp.float32) for shape in grads]
        + [pltpu.SemaphoreType.DMA((6,)), pltpu.SemaphoreType.DMA((5, 2))],
        compiler_params=pltpu.CompilerParams(vmem_limit_bytes=60 << 20),
        name="finish",
    )(sums, output, grad_tokens)


def chip_body(tokens, w_qkv, w_out, doc_blocks, cotangent):
    n = lax.axis_size("fsdp")
    all_devices = lax.axis_size("dp") * n
    sums, output, grad_tokens = layer(n, tokens, cotangent, w_qkv, w_out, doc_blocks)
    norm_factor = 1.0 / math.sqrt(tokens.shape[0] * all_devices)
    return tuple(finish(norm_factor, sums, output, grad_tokens))


def solution(mesh):
    placed = (
        P(("dp", "fsdp"), None),
        P("fsdp", None),
        P("fsdp", None),
        P(("dp", "fsdp"), None),
        P(("dp", "fsdp"), None),
    )
    in_plane = mesh.shape["dp"] == 8 and mesh.shape["fsdp"] == 4
    return jax.shard_map(
        chip_body if in_plane else body,
        mesh=mesh,
        in_specs=placed,
        out_specs=(
            P(("dp", "fsdp"), None),
            P(("dp", "fsdp"), None),
            P("fsdp", None),
            P("fsdp", None),
        ),
        check_vma=False,
    )
```
